32 devices in a mesh: grp: 2 (over y), ctx: 4 (over x, core), head: 4 (over z).
Axes of the slice: x: 2, y: 2, z: 4, core: 2. Of those that a mesh axis runs over, the one named last changes fastest.
Arguments:
- query_codes: bfloat16 [8192, 2048], P(('grp', 'ctx', 'head')), parts along dimension 0, may hold values from -0.5 to 2.5
- key_codes: bfloat16 [8192, 2048], P(('grp', 'ctx', 'head')), parts along dimension 0, may hold values from -0.5 to 2.5
- value_codes: bfloat16 [8192, 4096], P(('grp', 'ctx', 'head')), parts along dimension 0, may hold values from -6 to 6
- block_scales: float32 [64, 3, 8], P(('grp', 'ctx', 'head')), parts along dimension 0, may hold values from 0.25 to 2
- fault_tensor: int32 [64, 8], P(('grp', 'ctx', 'head')), parts along dimension 0, may hold values from 0 to 2
- fault_offset: int32 [64, 8], P(('grp', 'ctx', 'head')), parts along dimension 0, may hold values from 0 to 65535
- fault_bit: int32 [64, 8], P(('grp', 'ctx', 'head')), parts along dimension 0, may hold values from 0 to 3
- input_gate: bfloat16 [8192, 8], P(('grp', 'ctx', 'head')), parts along dimension 0, may hold values from -10 to 104
- forget_gate: bfloat16 [8192, 8], P(('grp', 'ctx', 'head')), parts along dimension 0, may hold values from 0.5 to 15
Outputs:
- hidden_states: bfloat16 [8192, 4096], P(('grp', 'ctx', 'head')), parts along dimension 0
The draws below stay inside these ranges and needn't reach their ends.
There are 2 independent parts, one for each index of `grp`. The reference program is written for one: setup_inputs(seed, part) draws one part's arguments, and reference() takes and returns one part's arrays. A program takes and returns all parts, laid end to end along the dimension named above; each array names one. Nothing has to cross between parts.
All inputs are finite; a program needn't handle non-finite values.
Results may differ from the reference program's by a relative error of at most 0.0057.
Values may be sent and summed in bfloat16 or wider, within the bound.
No kernel may reach another device: no remote copies, remote signals or barrier semaphores. Data moves between devices by JAX's collectives and lax.ppermute only.
A program may use at most 128 MiB of HBM per device.

```python
import math
import jax
import jax.numpy as jnp
from jax import lax

ATTENTION_UNITS = 8
DK = 256
DV = 512
CH = 256
BLK = 128
CONTEXT_LENGTH = 4096
NBLK = 32


def shared_codes(key):
    spanwise_outcome = 0.5 * jnp.clip(jax.random.normal(key, (CONTEXT_LENGTH, ATTENTION_UNITS * DK)), -3.0, 3.0)
    return (1.0 + spanwise_outcome).astype(jnp.bfloat16)


def draw_query_codes(key, part):
    return shared_codes(jax.random.fold_in(key, 11))


def draw_key_codes(key, part):
    return shared_codes(jax.random.fold_in(key, 23))


def draw_input_gate(key, part):
    return jnp.clip(-2.0 + 1.5 * jax.random.normal(key, (CONTEXT_LENGTH, ATTENTION_UNITS)), -10.0, 6.0).astype(jnp.bfloat16)


def draw_forget_gate(key, part):
    lookup_vectors = jax.random.split(key, 6)
    order = jax.random.permutation(lookup_vectors[0], ATTENTION_UNITS)
    quick = order < ATTENTION_UNITS // 2
    slow_base = jnp.minimum(math.log(CONTEXT_LENGTH) + 1.0 + jax.random.uniform(lookup_vectors[1], (ATTENTION_UNITS,), minval=0.0, maxval=2.0), 14.0)
    quick_base = math.log(40.0) + jax.random.uniform(lookup_vectors[2], (ATTENTION_UNITS,), minval=-0.3, maxval=0.3)
    drawn_outcome = jnp.where(quick, quick_base, slow_base)
    spanwise_outcome = jax.random.uniform(lookup_vectors[3], (CONTEXT_LENGTH, ATTENTION_UNITS), minval=-0.35, maxval=0.35)
    corruption_positions = jax.random.randint(lookup_vectors[4], (3,), 0, CONTEXT_LENGTH)
    corruption_cluster = jnp.any(jnp.arange(CONTEXT_LENGTH)[:, None] == corruption_positions[None, :], axis=1)
    corruption_cluster_amount = jax.random.uniform(lookup_vectors[5], (CONTEXT_LENGTH, ATTENTION_UNITS), minval=0.7, maxval=1.4)
    return jnp.where(corruption_cluster[:, None], corruption_cluster_amount, drawn_outcome[None, :] + spanwise_outcome).astype(jnp.bfloat16)


def touch_ends(values, key, least, top_value):
    index_at = [jax.random.randint(jax.random.fold_in(key, axis), (), 0, length) for axis, length in enumerate(values.shape)]
    main_axis = values.shape.index(max(values.shape))
    beside = index_at[:main_axis] + [(index_at[main_axis] + 1) % values.shape[main_axis]] + index_at[main_axis + 1:]
    return values.at[tuple(index_at)].set(least).at[tuple(beside)].set(top_value)


def shard_levels(stream_key, shape, cuts, smallest, top_value):
    level = 1.0
    for axis_at, blocks in cuts:
        heights = jax.random.uniform(jax.random.fold_in(jax.random.fold_in(stream_key, 6), axis_at), (blocks,), jnp.float32, smallest / len(cuts), top_value / len(cuts))
        level = level * jnp.repeat(jnp.exp(heights), shape[axis_at] // blocks).reshape((-1,) + (1,) * (len(shape) - 1 - axis_at))
    return level


def bell_draw(stream_key, shape, scale, bound, cuts=(), kind=jnp.bfloat16):
    values = jax.random.normal(stream_key, shape, jnp.float32) * scale
    if len(cuts) > 0:
        values = shard_levels(stream_key, shape, cuts, -0.22, 0.18) * values
    return jnp.clip(values, min=-bound, max=bound).astype(kind)


def setup_inputs(seed: int = 0, part: int = 0) -> dict:
    key_list = jax.random.split(jax.random.key(seed), 10)
    own_keys = jax.random.split(jax.random.fold_in(key_list[9], part), 10)
    query_codes = draw_query_codes(jax.random.fold_in(jax.random.fold_in(key_list[9], part), 71), part)
    key_codes = draw_key_codes(jax.random.fold_in(jax.random.fold_in(key_list[9], part), 71), part)
    value_codes = bell_draw(own_keys[2], (CONTEXT_LENGTH, ATTENTION_UNITS * DV), 1.0, 6.0, ((0, 16),))
    block_scales = jnp.clip(jnp.exp(math.log(2.0) - 2.0794415 * jax.random.uniform(own_keys[3], (NBLK, 3, ATTENTION_UNITS), jnp.float32) ** shard_levels(own_keys[3], (NBLK, 3, ATTENTION_UNITS), ((0, 16),), -0.2, 0.2)), 0.25, 2.0)
    fault_tensor = touch_ends(jax.random.randint(own_keys[4], (NBLK, ATTENTION_UNITS), 0, 3), jax.random.fold_in(own_keys[4], 1), 0, 2).astype(jnp.int32)
    fault_offset = touch_ends(jax.random.randint(own_keys[5], (NBLK, ATTENTION_UNITS), 0, BLK * DV), jax.random.fold_in(own_keys[5], 1), 0, (BLK * DV) - 1).astype(jnp.int32)
    fault_bit = touch_ends(jax.random.randint(own_keys[6], (NBLK, ATTENTION_UNITS), 0, 4), jax.random.fold_in(own_keys[6], 1), 0, 3).astype(jnp.int32)
    input_gate = draw_input_gate(jax.random.fold_in(jax.random.fold_in(key_list[9], part), 71), part)
    forget_gate = draw_forget_gate(jax.random.fold_in(jax.random.fold_in(key_list[9], part), 71), part)
    return dict(query_codes=query_codes, key_codes=key_codes, value_codes=value_codes, block_scales=block_scales, fault_tensor=fault_tensor, fault_offset=fault_offset, fault_bit=fault_bit, input_gate=input_gate, forget_gate=forget_gate)


NEG_FILL = -1e+30

def dequant(codes, scales, tensor_id, fault_tensor, fault_offset, fault_bit, width):
    rows = codes.shape[0]
    blocks = rows // BLK
    heads = scales.shape[2]
    shaped = codes.reshape(blocks, BLK, heads, width).astype(jnp.float32)
    block_factor = scales[:, tensor_id, :]
    struck = fault_tensor == tensor_id
    token_hit = (fault_offset // DV).astype(jnp.int32)
    column_hit = (fault_offset % DV % width).astype(jnp.int32)
    token_line = jnp.arange(BLK, dtype=jnp.int32)
    column_line = jnp.arange(width, dtype=jnp.int32)
    marked = (token_line[None, :, None, None] == token_hit[:, None, :, None]) & (column_line[None, None, None, :] == column_hit[:, None, :, None]) & struck[:, None, :, None]
    flipped = -jnp.exp2(fault_bit.astype(jnp.float32))
    factor = jnp.where(marked, flipped[:, None, :, None], jnp.ones_like(shaped))
    result = shaped * block_factor[:, None, :, None] * factor
    return result.reshape(rows, heads, width).astype(jnp.bfloat16)

def identity_state(groups):
    return (jnp.zeros((groups, DK, DV), jnp.float32), jnp.zeros((groups, DK), jnp.float32), jnp.full((groups,), NEG_FILL, jnp.float32), jnp.zeros((groups,), jnp.float32))

def combine(earlier, following):
    peak = jnp.maximum(earlier[2] + following[3], following[2])
    first = jnp.exp(earlier[2] + following[3] - peak)
    second = jnp.exp(following[2] - peak)
    matrix = earlier[0] * first[..., None, None] + following[0] * second[..., None, None]
    normer = earlier[1] * first[..., None] + following[1] * second[..., None]
    return (matrix, normer, peak, earlier[3] + following[3])

def span_terms(lookup_vectors, values, gate_in, log_forget):
    running = jnp.cumsum(log_forget, axis=1)
    total = running[:, -1]
    exponent = total[:, None] - running + gate_in
    peak = lax.optimization_barrier(jnp.max(exponent, axis=1))
    weights = jnp.exp(exponent - peak[:, None])
    weighted = lax.optimization_barrier((lookup_vectors.astype(jnp.float32) * weights[..., None]).astype(jnp.bfloat16))
    wide = weighted.astype(jnp.float32)
    matrix = jnp.einsum('csgk,csgv->cgkv', wide, values.astype(jnp.float32))
    normer = lax.optimization_barrier(jnp.sum(wide, axis=1))
    return (matrix, normer, peak, total)

def prefix_states(states, start):

    def advance(carried, element):
        return (combine(carried, element), carried)
    return lax.scan(advance, start, states)

def span_outputs(queries, lookup_vectors, values, gate_in, log_forget, before):
    size = queries.shape[1]
    factor = 1.0 / math.sqrt(DK)
    running = jnp.cumsum(log_forget, axis=1).transpose(0, 2, 1)
    gate_rows = gate_in.transpose(0, 2, 1)
    exponent = running[..., :, None] - running[..., None, :] + gate_rows[..., None, :]
    line = jnp.arange(size, dtype=jnp.int32)
    causal = line[:, None] >= line[None, :]
    exponent = jnp.where(causal, exponent, NEG_FILL)
    inter = running + before[2][..., None]
    row_peak = jnp.maximum(lax.optimization_barrier(jnp.max(exponent, axis=-1)), inter)
    decay = jnp.exp(exponent - row_peak[..., None])
    scores = jnp.einsum('ctgk,csgk->cgts', queries.astype(jnp.float32), lookup_vectors.astype(jnp.float32)) * factor
    product = decay * scores
    product_weights = lax.optimization_barrier(product.astype(jnp.bfloat16))
    numerator = jnp.einsum('cgts,csgv->ctgv', product_weights.astype(jnp.float32), values.astype(jnp.float32))
    lift = jnp.exp(inter - row_peak)
    lifted = lax.optimization_barrier((queries.astype(jnp.float32) * (factor * lift).transpose(0, 2, 1)[..., None]).astype(jnp.bfloat16))
    start_matrix = lax.optimization_barrier(before[0].astype(jnp.bfloat16))
    numerator = numerator + jnp.einsum('ctgk,cgkv->ctgv', lifted.astype(jnp.float32), start_matrix.astype(jnp.float32))
    denominator = lax.optimization_barrier(jnp.sum(product, axis=-1)) + jnp.einsum('ctgk,cgk->cgt', lifted.astype(jnp.float32), before[1], precision=lax.Precision.HIGHEST)
    floor_value = jnp.maximum(jnp.abs(denominator), 1.0)
    return (numerator / floor_value.transpose(0, 2, 1)[..., None]).astype(jnp.bfloat16)

def reference(query_codes, key_codes, value_codes, block_scales, fault_tensor, fault_offset, fault_bit, input_gate, forget_gate):
    queries = dequant(query_codes, block_scales, 0, fault_tensor, fault_offset, fault_bit, DK)
    lookup_vectors = dequant(key_codes, block_scales, 1, fault_tensor, fault_offset, fault_bit, DK)
    values = dequant(value_codes, block_scales, 2, fault_tensor, fault_offset, fault_bit, DV)
    spans = CONTEXT_LENGTH // CH
    log_forget = jax.nn.log_sigmoid(forget_gate.astype(jnp.float32))
    gate_in = input_gate.astype(jnp.float32)

    def split_wide(array):
        return array.reshape(spans, CH, ATTENTION_UNITS, array.shape[2]).transpose(2, 0, 1, 3)[:, :, :, None, :]

    def split_gate(array):
        return array.reshape(spans, CH, ATTENTION_UNITS).transpose(2, 0, 1)[..., None]

    def head_pass(pieces):
        head_q, head_k, head_v, head_i, head_f = pieces
        terms = span_terms(head_k, head_v, head_i, head_f)
        total, before = prefix_states(terms, identity_state(1))
        return span_outputs(head_q, head_k, head_v, head_i, head_f, before)
    outputs = lax.map(head_pass, (split_wide(queries), split_wide(lookup_vectors), split_wide(values), split_gate(gate_in), split_gate(log_forget)))
    return outputs[:, :, :, 0, :].transpose(1, 2, 0, 3).reshape(CONTEXT_LENGTH, ATTENTION_UNITS * DV)
```

```python
import functools
import math

import jax
import jax.numpy as jnp
from jax import lax
from jax.experimental import pallas as pl
from jax.experimental.pallas import tpu as pltpu
from jax.sharding import PartitionSpec as P

DK = 256
DV = 512
CH = 256
BLK = 128
NEG_FILL = -1e30
TAIL = 8
ROWS = DK + TAIL
CHUNKS = (1, 1, 1, 1)

F32 = jnp.float32
BF16 = jnp.bfloat16


def sizes(mesh):
    ctx, head = mesh.shape["ctx"], mesh.shape["head"]
    head_bits, ctx_bits = head.bit_length() - 1, ctx.bit_length() - 1
    assert head == 1 << head_bits and ctx == 1 << ctx_bits and head_bits >= 1
    return head_bits, ctx_bits


def flip(x, bit, head_bits, ctx_bits, last):
    axis, size, b = (
        ("head", 1 << head_bits, bit) if bit < head_bits else ("ctx", 1 << ctx_bits, bit - head_bits)
    )
    pairs = [(i, i ^ (1 << b)) for i in range(size) if not (last and i & (1 << b))]
    return lax.ppermute(x, axis, pairs)


def span_index(head_bits):
    return lax.axis_index("ctx") * (1 << head_bits) + lax.axis_index("head")


def gate_kernel(i_ref, f_ref, run_ref, shift_ref, weight_ref, mf_ref):
    gate = i_ref[...].astype(F32)
    x = f_ref[...].astype(F32)
    log_forget = jnp.minimum(x, 0.0) - jnp.log1p(jnp.exp(-jnp.abs(x)))
    size = x.shape[0]
    row = lax.broadcasted_iota(jnp.int32, (size, size), 0)
    col = lax.broadcasted_iota(jnp.int32, (size, size), 1)
    below = jnp.where(row >= col, 1.0, 0.0).astype(F32)
    running = jnp.dot(below, log_forget, precision=lax.Precision.HIGHEST, preferred_element_type=F32)
    total = running[size - 1 : size, :]
    shift = gate - running
    exponent = total + shift
    peak = jnp.max(exponent, axis=0, keepdims=True)
    run_ref[...] = running
    shift_ref[...] = shift
    weight_ref[...] = jnp.exp(exponent - peak)
    mf_ref[...] = jnp.concatenate([peak, total], axis=0)


def gates(input_gate, forget_gate):
    size, heads = input_gate.shape
    col = jax.ShapeDtypeStruct((size, heads), F32)
    return pl.pallas_call(
        gate_kernel,
        out_shape=(col, col, col, jax.ShapeDtypeStruct((2, heads), F32)),
        name="gates",
    )(input_gate, forget_gate)


def coef_layout(bits):
    at, send = 0, {}
    for b in range(1, bits):
        send[b] = at
        at += 1 + b
    own, other, peak = at, at + bits, at + 2 * bits
    return send, own, other, peak, peak + 1


def coef_kernel(head_bits, bits, tab_ref, out_ref):
    spans = 1 << bits
    me = span_index(head_bits)
    peaks = tab_ref[pl.ds(0, spans, stride=2), :]
    totals = tab_ref[pl.ds(1, spans, stride=2), :]
    j = lax.broadcasted_iota(jnp.int32, (spans, 1), 0) ^ me
    j_row = lax.broadcasted_iota(jnp.int32, (1, spans), 1) ^ me
    upto = jnp.where(j_row <= j, 1.0, 0.0).astype(F32)
    running = jnp.dot(upto, totals, precision=lax.Precision.HIGHEST, preferred_element_type=F32)
    level = peaks - running

    def top(mask):
        return jnp.max(jnp.where(mask, level, NEG_FILL), axis=0, keepdims=True)

    def weight(a, b):
        return jnp.exp(jnp.minimum(a - b, 0.0))

    group = [top((j >> b) == (me >> b)) for b in range(bits)]
    peer = [top((j >> b) == ((me >> b) ^ 1)) for b in range(bits)]
    bit = [((me >> b) & 1) == 1 for b in range(bits)]
    zero = jnp.zeros_like(group[0])
    rows = []
    for b in range(1, bits):
        rows.append(weight(group[0], group[b]))
        rows += [weight(peer[k], group[b]) for k in range(b)]
    mine, theirs = top(j < me), top(j < (me ^ 1))
    rows += [jnp.where(bit[b], weight(peer[b], mine), zero) for b in range(bits)]
    rows.append(jnp.where(bit[0], zero, weight(group[0], theirs)))
    rows += [jnp.where(bit[b], weight(peer[b], theirs), zero) for b in range(1, bits)]
    before = jnp.sum(jnp.where(j < me, totals, 0.0), axis=0, keepdims=True)
    rows.append(jnp.where(me > 0, before + mine, NEG_FILL))
    for r, value in enumerate(rows):
        out_ref[r : r + 1, :] = value


def coefficients(table, head_bits, bits):
    rows = coef_layout(bits)[-1]
    return pl.pallas_call(
        functools.partial(coef_kernel, head_bits, bits),
        out_shape=jax.ShapeDtypeStruct((rows, table.shape[1]), F32),
        name="coefficients",
    )(table)


def pick(ref, h):
    x = ref[...]
    lane = lax.broadcasted_iota(jnp.int32, x.shape, 1)
    return jnp.sum(jnp.where(lane == h, x, 0.0), axis=1, keepdims=True)


def dequant(codes, tensor_id, h, scales, tensors, offsets, bits):
    rows, width = codes.shape
    x = codes.astype(F32)
    row = lax.broadcasted_iota(jnp.int32, (rows, 1), 0)
    col = lax.broadcasted_iota(jnp.int32, (1, width), 1)
    scale = jnp.zeros((rows, 1), F32)
    for b in range(rows // BLK):
        scale = jnp.where(row // BLK == b, scales[b, tensor_id, h], scale)
    x = x * scale
    for b in range(rows // BLK):
        offset = offsets[b, h]
        hit_row = jnp.where(tensors[b, h] == tensor_id, b * BLK + offset // DV, -1)
        hit_col = (offset % DV) % width
        flipped = -(lax.shift_left(jnp.int32(1), bits[b, h]).astype(F32))
        x = jnp.where((row == hit_row) & (col == hit_col), x * flipped, x)
    return x.astype(BF16)


def pack_tail(n):
    high = n.astype(BF16).astype(F32)
    low = (n - high).astype(BF16).astype(F32)
    least = n - high - low
    first = jnp.concatenate([high, low], axis=1)
    second = jnp.concatenate([least, jnp.zeros_like(least)], axis=1)
    row = lax.broadcasted_iota(jnp.int32, (TAIL, DV), 0)
    return jnp.where(row == 0, first, jnp.where(row == 1, second, 0.0)).astype(BF16)


def read_tail(ref, i):
    t = ref[i, DK:ROWS, :].astype(F32)
    return t[0:1, :DK] + t[0:1, DK : 2 * DK] + t[1:2, :DK]


def state_kernel(first, scales, tensors, offsets, fbits, weight_ref, k_ref, v_ref, keep_ref, send_ref):
    own = lax.axis_index("head") & 1
    pair = first + pl.program_id(0)
    for out_ref, side in ((send_ref, 1 - own), (keep_ref, own)):
        h = 2 * pair + side
        info = (h, scales, tensors, offsets, fbits)
        k = dequant(k_ref[:, pl.ds(pl.multiple_of(side * DK, DK), DK)], 1, *info)
        v = dequant(v_ref[:, pl.ds(pl.multiple_of(side * DV, DV), DV)], 2, *info)
        weighted = (k.astype(F32) * pick(weight_ref, h)).astype(BF16)
        matrix = lax.dot_general(weighted, v, (((0,), (0,)), ((), ())), preferred_element_type=F32)
        out_ref[0, :DK, :] = matrix.astype(BF16)
        out_ref[0, DK:ROWS, :] = pack_tail(jnp.sum(weighted.astype(F32), axis=0, keepdims=True))


SMEM = pl.BlockSpec(memory_space=pltpu.SMEM)


def whole(shape):
    return pl.BlockSpec(shape, lambda i: (0,) * len(shape))


STATE = pl.BlockSpec((1, ROWS, DV), lambda i: (i, 0, 0))


def span_states(first, count, small, weight, key_codes, value_codes):
    rows = key_codes.shape[0]
    out = jax.ShapeDtypeStruct((count, ROWS, DV), BF16)
    return pl.pallas_call(
        functools.partial(state_kernel, first),
        grid=(count,),
        in_specs=[SMEM] * 4
        + [
            whole(weight.shape),
            pl.BlockSpec((rows, 2 * DK), lambda i: (0, first + i)),
            pl.BlockSpec((rows, 2 * DV), lambda i: (0, first + i)),
        ],
        out_specs=(STATE, STATE),
        out_shape=(out, out),
        cost_estimate=pl.CostEstimate(
            flops=count * 4 * rows * DK * DV, bytes_accessed=count * rows * 2 * (2 * DK + 4 * DV), transcendentals=0
        ),
        name="span_states",
    )(*small, weight, key_codes, value_codes)


def combined(coefs, h, at, refs):
    total, normer = None, None
    for r, ref in zip(at, refs):
        c = coefs[r, h]
        term, tail = ref[0, :DK, :].astype(F32) * c, read_tail(ref, 0) * c
        total = term if total is None else total + term
        normer = tail if normer is None else normer + tail
    return total, normer


def combine_kernel(first, at, coefs, *refs):
    h = 2 * (first + pl.program_id(0)) + (lax.axis_index("head") & 1)
    total, normer = combined(coefs, h, at, refs[:-1])
    refs[-1][0, :DK, :] = total.astype(BF16)
    refs[-1][0, DK:ROWS, :] = pack_tail(normer)


def combine(first, at, coefs, parts):
    count = parts[0].shape[0]
    return pl.pallas_call(
        functools.partial(combine_kernel, first, at),
        grid=(count,),
        in_specs=[SMEM] + [STATE] * len(parts),
        out_specs=STATE,
        out_shape=jax.ShapeDtypeStruct((count, ROWS, DV), BF16),
        cost_estimate=pl.CostEstimate(
            flops=count * ROWS * DV * 2 * len(parts), bytes_accessed=count * ROWS * DV * 2 * (len(parts) + 1), transcendentals=0
        ),
        name="combine",
    )(coefs, *parts)


def output_kernel(
    first, at, peak_row, has_out, coefs, scales, tensors, offsets, fbits, run_ref, shift_ref, q_ref, k_ref, v_ref, back_ref, *rest
):
    parts, out_ref = rest[: len(at)], rest[-1]
    own = lax.axis_index("head") & 1
    pair = first + pl.program_id(0)
    factor = 1.0 / math.sqrt(DK)
    size = q_ref.shape[0]
    row = lax.broadcasted_iota(jnp.int32, (size, size), 0)
    col = lax.broadcasted_iota(jnp.int32, (size, size), 1)
    for side, mine in ((own, True), (1 - own, False)):
        h = 2 * pair + side
        info = (h, scales, tensors, offsets, fbits)
        if mine:
            start, normer = combined(coefs, h, at, parts)
            start = start.astype(BF16)
        else:
            start, normer = back_ref[0, :DK, :], read_tail(back_ref, 0)
        narrow = pl.ds(pl.multiple_of(side * DK, DK), DK)
        wide = pl.ds(pl.multiple_of(side * DV, DV), DV)
        q = dequant(q_ref[:, narrow], 0, *info)
        k = dequant(k_ref[:, narrow], 1, *info)
        v = dequant(v_ref[:, wide], 2, *info)
        run, shift = pick(run_ref, h), pick(shift_ref, h)
        shift_row = jnp.sum(jnp.where(row == col, shift, 0.0), axis=0, keepdims=True)
        exponent = jnp.where(row >= col, run + shift_row, NEG_FILL)
        inter = run + coefs[peak_row, h]
        row_peak = jnp.maximum(jnp.max(exponent, axis=1, keepdims=True), inter)
        decay = jnp.exp(exponent - row_peak)
        scores = lax.dot_general(q, k, (((1,), (1,)), ((), ())), preferred_element_type=F32) * factor
        product = decay * scores
        lifted = (q.astype(F32) * (factor * jnp.exp(inter - row_peak))).astype(BF16)
        numerator = jnp.dot(product.astype(BF16), v, preferred_element_type=F32)
        numerator = numerator + jnp.dot(lifted, start, preferred_element_type=F32)
        denominator = jnp.sum(product, axis=1, keepdims=True) + jnp.sum(
            lifted.astype(F32) * normer, axis=1, keepdims=True
        )
        out_ref[:, wide] = (numerator / jnp.maximum(jnp.abs(denominator), 1.0)).astype(BF16)


def span_outputs(first, at, peak_row, coefs, small, run, shift, codes, back, parts, before):
    q, k, v = codes
    count, rows = back.shape[0], q.shape[0]
    narrow = pl.BlockSpec((rows, 2 * DK), lambda i: (0, first + i))
    wide = pl.BlockSpec((rows, 2 * DV), lambda i: (0, first + i))
    operands = [coefs, *small, run, shift, q, k, v, back, *parts]
    in_specs = [SMEM] * 5 + [whole(run.shape)] * 2 + [narrow, narrow, wide, STATE] + [STATE] * len(parts)
    aliases = {}
    if before is not None:
        aliases = {len(operands): 0}
        operands.append(before)
        in_specs.append(pl.BlockSpec(memory_space=pl.ANY))
    return pl.pallas_call(
        functools.partial(output_kernel, first, at, peak_row, before is not None),
        grid=(count,),
        in_specs=in_specs,
        out_specs=wide,
        out_shape=jax.ShapeDtypeStruct(v.shape, BF16),
        input_output_aliases=aliases,
        cost_estimate=pl.CostEstimate(
            flops=count * 4 * rows * (rows * DK + rows * DV + DK * DV),
            bytes_accessed=count * (rows * 2 * (4 * DK + 4 * DV) + ROWS * DV * 2 * (1 + len(parts))),
            transcendentals=count * 2 * rows * rows,
        ),
        name="span_outputs",
    )(*operands)


def body(
    head_bits,
    ctx_bits,
    query_codes,
    key_codes,
    value_codes,
    block_scales,
    fault_tensor,
    fault_offset,
    fault_bit,
    input_gate,
    forget_gate,
):
    bits = head_bits + ctx_bits
    assert query_codes.shape[0] == CH
    send_at, own_at, other_at, peak_row, _ = coef_layout(bits)
    small = (block_scales, fault_tensor, fault_offset, fault_bit)
    exchange = functools.partial(flip, head_bits=head_bits, ctx_bits=ctx_bits)
    run, shift, weight, table = gates(input_gate, forget_gate)
    for b in range(bits):
        table = jnp.concatenate([table, exchange(table, b, last=False)], axis=0)
    coefs = coefficients(table, head_bits, bits)

    starts = [sum(CHUNKS[:c]) for c in range(len(CHUNKS))]
    assert 2 * sum(CHUNKS) == input_gate.shape[1]
    out = None
    for first, count in zip(starts, CHUNKS):
        keep, send = span_states(first, count, small, weight, key_codes, value_codes)
        got = [exchange(send, 0, last=False)]
        for b in range(1, bits):
            at = [send_at[b] + r for r in range(b + 1)]
            group = combine(first, at, coefs, [keep, *got])
            got.append(exchange(group, b, last=b == bits - 1))
        at = [other_at + r for r in range(bits)]
        back = exchange(combine(first, at, coefs, [keep, *got[1:]]), 0, last=False)
        at = [own_at + r for r in range(bits)]
        out = span_outputs(
            first, at, peak_row, coefs, small, run, shift, (query_codes, key_codes, value_codes), back, got, out
        )
    return out


def solution(mesh):
    rows = P(("grp", "ctx", "head"), None)
    placed = (rows, rows, rows, P(("grp", "ctx", "head"), None, None)) + (rows,) * 5
    return jax.shard_map(
        functools.partial(body, *sizes(mesh)), mesh=mesh, in_specs=placed, out_specs=rows, check_vma=False
    )
```

```python
import functools
import math

import jax
import jax.numpy as jnp
from jax import lax
from jax.experimental import pallas as pl
from jax.experimental.pallas import tpu as pltpu
from jax.sharding import PartitionSpec as P

DK = 256
DV = 512
CH = 256
BLK = 128
NEG_FILL = -1e30
TAIL = 8
ROWS = DK + TAIL
CHUNKS = (1, 1, 1, 1)

F32 = jnp.float32
BF16 = jnp.bfloat16


def sizes(mesh):
    ctx, head = mesh.shape["ctx"], mesh.shape["head"]
    head_bits, ctx_bits = head.bit_length() - 1, ctx.bit_length() - 1
    assert head == 1 << head_bits and ctx == 1 << ctx_bits and head_bits >= 1
    return head_bits, ctx_bits


def flip(x, bit, head_bits, ctx_bits, last):
    axis, size, b = (
        ("head", 1 << head_bits, bit) if bit < head_bits else ("ctx", 1 << ctx_bits, bit - head_bits)
    )
    pairs = [(i, i ^ (1 << b)) for i in range(size) if not (last and i & (1 << b))]
    return lax.ppermute(x, axis, pairs)


def gate_kernel(i_ref, f_ref, run_ref, weight_ref, shift_ref, mf_ref):
    gate, x = i_ref[...], f_ref[...].astype(F32)
    log_forget = jnp.minimum(x, 0.0) - jnp.log1p(jnp.exp(-jnp.abs(x)))
    size = x.shape[1]
    row = lax.broadcasted_iota(jnp.int32, (size, size), 0)
    col = lax.broadcasted_iota(jnp.int32, (size, size), 1)
    before = jnp.where(row >= col, 1.0, 0.0).astype(F32)
    same = jnp.where(row == col, 1.0, 0.0).astype(BF16)
    exact = dict(precision=lax.Precision.HIGHEST, preferred_element_type=F32)
    across = (((1,), (1,)), ((), ()))
    running_row = lax.dot_general(log_forget, before, across, **exact)
    running = lax.dot_general(before, log_forget, across, **exact)
    gate_col = lax.dot_general(same, gate, across, preferred_element_type=F32)
    total = running[size - 1 : size, :]
    exponent = total - running + gate_col
    peak = jnp.max(exponent, axis=0, keepdims=True)
    run_ref[...] = running
    weight_ref[...] = jnp.exp(exponent - peak)
    shift_ref[...] = gate.astype(F32) - running_row
    mf_ref[...] = jnp.concatenate([peak, total], axis=0)


def gates(input_gate, forget_gate):
    heads, size = input_gate.shape
    col = jax.ShapeDtypeStruct((size, heads), F32)
    row = jax.ShapeDtypeStruct((heads, size), F32)
    return pl.pallas_call(
        gate_kernel,
        out_shape=(col, col, row, jax.ShapeDtypeStruct((2, heads), F32)),
        compiler_params=pltpu.CompilerParams(vmem_limit_bytes=4 << 20),
        cost_estimate=pl.CostEstimate(flops=1 << 20, bytes_accessed=1 << 20, transcendentals=0),
        name="gates",
    )(input_gate, forget_gate)


def pick(ref, h):
    x = ref[...]
    lane = lax.broadcasted_iota(jnp.int32, x.shape, 1)
    return jnp.sum(jnp.where(lane == h, x, 0.0), axis=1, keepdims=True)


def dequant(ref, at, width, tensor_id, h, scales, tensors, offsets, bits):
    rows = ref.shape[0]
    row = lax.broadcasted_iota(jnp.int32, (BLK, 1), 0)
    col = lax.broadcasted_iota(jnp.int32, (1, width), 1)
    out = []
    for b in range(rows // BLK):
        x = ref[b * BLK : (b + 1) * BLK, pl.ds(at, width)].astype(F32)
        offset, scale = offsets[b, h], scales[tensor_id, b, h]
        hit_row = jnp.where(tensors[b, h] == tensor_id, offset // DV, -1)
        hit_col = (offset % DV) % width
        flipped = -(lax.shift_left(jnp.int32(1), bits[b, h]).astype(F32)) * scale
        out.append((x * jnp.where((row == hit_row) & (col == hit_col), flipped, scale)).astype(BF16))
    return jnp.concatenate(out, axis=0)


def split(x):
    high = x.astype(BF16).astype(F32)
    middle = (x - high).astype(BF16).astype(F32)
    return high, middle, x - high - middle


def pack_tail(normer, peak, total):
    high, middle, least = split(normer)
    rows = [jnp.concatenate([high, middle], axis=1), jnp.concatenate([least, jnp.zeros_like(least)], axis=1)]
    rows += [*split(peak), *split(total)]
    at = lax.broadcasted_iota(jnp.int32, (TAIL, DV), 0)
    out = jnp.zeros((TAIL, DV), F32)
    for r, value in enumerate(rows):
        out = jnp.where(at == r, value, out)
    return out.astype(BF16)


class State:
    def __init__(self, ref, i):
        self.ref, self.i = ref, i
        t = ref[i, DK:ROWS, :].astype(F32)
        self.normer = t[0:1, :DK] + t[0:1, DK : 2 * DK] + t[1:2, :DK]
        self.peak = t[2:3] + t[3:4] + t[4:5]
        self.total = t[5:6] + t[6:7] + t[7:8]

    def matrix(self):
        return self.ref[self.i, :DK, :]


def joined(early, late):
    peak = jnp.maximum(early[0] + late[1], late[0])
    return peak, early[1] + late[1], jnp.exp(early[0] + late[1] - peak), jnp.exp(late[0] - peak)


def group_weights(bit, own, got):
    peak, total, weights = own.peak, own.total, [jnp.ones_like(own.peak)]
    for b, peer in enumerate(got):
        low = joined((peak, total), (peer.peak, peer.total))
        high = joined((peer.peak, peer.total), (peak, total))
        peak, total = jnp.where(bit[b], high[0], low[0]), low[1]
        here, there = jnp.where(bit[b], high[3], low[2]), jnp.where(bit[b], high[2], low[3])
        weights = [w * here for w in weights] + [there]
    return weights, peak, total


def start_weights(bit, include, own, got):
    peak, total, weights = None, None, []
    one = jnp.ones_like(got[-1].peak)
    peak, total = one * NEG_FILL, one * 0.0
    if own is not None:
        peak, total = jnp.where(include, own.peak, peak), jnp.where(include, own.total, total)
        weights = [jnp.where(include, one, 0.0)]
    for b, peer in zip(range(len(bit) - len(got), len(bit)), got):
        new = joined((peer.peak, peer.total), (peak, total))
        weights = [w * jnp.where(bit[b], new[3], 1.0) for w in weights] + [jnp.where(bit[b], new[2], 0.0)]
        peak, total = jnp.where(bit[b], new[0], peak), jnp.where(bit[b], new[1], total)
    return weights, peak, total


def weighted_sum(weights, states):
    matrix, normer = None, None
    for w, state in zip(weights, states):
        term, tail = state.matrix().astype(F32) * w, state.normer * w[:, :DK]
        matrix = term if matrix is None else matrix + term
        normer = tail if normer is None else normer + tail
    return matrix, normer


def device_bits(head_bits, bits):
    me = lax.axis_index("ctx") * (1 << head_bits) + lax.axis_index("head")
    return [((me >> b) & 1) == 1 for b in range(bits)]


SMEM = pl.BlockSpec(memory_space=pltpu.SMEM)
VMEM = pl.BlockSpec(memory_space=pltpu.VMEM)


def state_kernel(first, scales, tensors, offsets, fbits, mf, weight_ref, k_ref, v_ref, keep_ref, send_ref):
    own = lax.axis_index("head") & 1
    i = pl.program_id(0)
    for out_ref, side in ((send_ref, 1 - own), (keep_ref, own)):
        h = 2 * (first + i) + side
        info = (h, scales, tensors, offsets, fbits)
        k = dequant(k_ref, pl.multiple_of(side * DK, DK), DK, 1, *info)
        v = dequant(v_ref, pl.multiple_of(side * DV, DV), DV, 2, *info)
        weighted = (k.astype(F32) * pick(weight_ref, h)).astype(BF16)
        matrix = lax.dot_general(weighted, v, (((0,), (0,)), ((), ())), preferred_element_type=F32)
        out_ref[0, :DK, :] = matrix.astype(BF16)
        normer = jnp.sum(weighted.astype(F32), axis=0, keepdims=True)
        out_ref[0, DK:ROWS, :] = pack_tail(normer, jnp.full((1, DV), mf[0, h], F32), jnp.full((1, DV), mf[1, h], F32))


def whole(shape):
    return pl.BlockSpec(shape, lambda i: (0,) * len(shape))


STATE = pl.BlockSpec((1, ROWS, DV), lambda i: (i, 0, 0))


def span_states(first, count, small, mf, weight, key_codes, value_codes):
    rows = key_codes.shape[0]
    out = jax.ShapeDtypeStruct((count, ROWS, DV), BF16)
    return pl.pallas_call(
        functools.partial(state_kernel, first),
        grid=(count,),
        in_specs=[SMEM] * 5
        + [
            whole(weight.shape),
            pl.BlockSpec((rows, 2 * DK), lambda i: (0, first + i)),
            pl.BlockSpec((rows, 2 * DV), lambda i: (0, first + i)),
        ],
        out_specs=(STATE, STATE),
        out_shape=(out, out),
        compiler_params=pltpu.CompilerParams(vmem_limit_bytes=12 << 20),
        cost_estimate=pl.CostEstimate(
            flops=count * 4 * rows * DK * DV, bytes_accessed=count * rows * 2 * (2 * DK + 4 * DV), transcendentals=0
        ),
        name="span_states",
    )(*small, mf, weight, key_codes, value_codes)


def combine_kernel(head_bits, bits, last, *refs):
    parts, out_ref = refs[:-1], refs[-1]
    bit = device_bits(head_bits, bits)
    for i in range(out_ref.shape[0]):
        states = [State(ref, i) for ref in parts]
        if last:
            weights, peak, total = start_weights(bit, jnp.logical_not(bit[0]), states[0], states[1:])
        else:
            weights, peak, total = group_weights(bit, states[0], states[1:])
        matrix, normer = weighted_sum(weights, states)
        out_ref[i, :DK, :] = matrix.astype(BF16)
        out_ref[i, DK:ROWS, :] = pack_tail(normer, peak, total)


def combine(head_bits, bits, last, parts):
    count = parts[0].shape[0]
    return pl.pallas_call(
        functools.partial(combine_kernel, head_bits, bits, last),
        in_specs=[VMEM] * len(parts),
        out_specs=VMEM,
        out_shape=jax.ShapeDtypeStruct((count, ROWS, DV), BF16),
        compiler_params=pltpu.CompilerParams(vmem_limit_bytes=8 << 20),
        cost_estimate=pl.CostEstimate(
            flops=count * ROWS * DV * 2 * len(parts), bytes_accessed=count * ROWS * DV * 2 * (len(parts) + 1), transcendentals=0
        ),
        name="combine",
    )(*parts)


def output_kernel(
    head_bits, bits, first, scales, tensors, offsets, fbits, run_ref, shift_ref, q_ref, k_ref, v_ref, back_ref, *rest
):
    parts, out_ref = rest[:bits], rest[-1]
    bit = device_bits(head_bits, bits)
    own = lax.axis_index("head") & 1
    i = pl.program_id(0)
    factor = 1.0 / math.sqrt(DK)
    size = q_ref.shape[0]
    row = lax.broadcasted_iota(jnp.int32, (size, size), 0)
    col = lax.broadcasted_iota(jnp.int32, (size, size), 1)
    for side, mine in ((own, True), (1 - own, False)):
        h = 2 * (first + i) + side
        info = (h, scales, tensors, offsets, fbits)
        if mine:
            states = [State(ref, 0) for ref in parts]
            weights, peak, _ = start_weights(bit, None, None, states)
            start, normer = weighted_sum(weights, states)
            start = start.astype(BF16)
        else:
            back = State(back_ref, 0)
            start, normer, peak = back.matrix(), back.normer, back.peak
        narrow, wide = pl.multiple_of(side * DK, DK), pl.multiple_of(side * DV, DV)
        q = dequant(q_ref, narrow, DK, 0, *info)
        k = dequant(k_ref, narrow, DK, 1, *info)
        v = dequant(v_ref, wide, DV, 2, *info)
        run = pick(run_ref, h)
        exponent = jnp.where(row >= col, run + shift_ref[pl.ds(h, 1), :], NEG_FILL)
        inter = run + peak[:, :1]
        row_peak = jnp.maximum(jnp.max(exponent, axis=1, keepdims=True), inter)
        decay = jnp.exp(exponent - row_peak)
        scores = lax.dot_general(q, k, (((1,), (1,)), ((), ())), preferred_element_type=F32) * factor
        product = decay * scores
        lifted = (q.astype(F32) * (factor * jnp.exp(inter - row_peak))).astype(BF16)
        numerator = jnp.dot(product.astype(BF16), v, preferred_element_type=F32)
        numerator = numerator + jnp.dot(lifted, start, preferred_element_type=F32)
        denominator = jnp.sum(product, axis=1, keepdims=True) + jnp.sum(
            lifted.astype(F32) * normer, axis=1, keepdims=True
        )
        out_ref[:, pl.ds(wide, DV)] = (numerator / jnp.maximum(jnp.abs(denominator), 1.0)).astype(BF16)


def span_outputs(head_bits, bits, first, small, run, shift, codes, back, parts, before):
    q, k, v = codes
    count, rows = back.shape[0], q.shape[0]
    narrow = pl.BlockSpec((rows, 2 * DK), lambda i: (0, first + i))
    wide = pl.BlockSpec((rows, 2 * DV), lambda i: (0, first + i))
    operands = [*small, run, shift, q, k, v, back, *parts]
    in_specs = [SMEM] * 4 + [whole(run.shape), whole(shift.shape)] + [narrow, narrow, wide, STATE] + [STATE] * len(parts)
    aliases = {}
    if before is not None:
        aliases = {len(operands): 0}
        operands.append(before)
        in_specs.append(pl.BlockSpec(memory_space=pl.ANY))
    return pl.pallas_call(
        functools.partial(output_kernel, head_bits, bits, first),
        grid=(count,),
        in_specs=in_specs,
        out_specs=wide,
        out_shape=jax.ShapeDtypeStruct(v.shape, BF16),
        input_output_aliases=aliases,
        compiler_params=pltpu.CompilerParams(vmem_limit_bytes=16 << 20),
        cost_estimate=pl.CostEstimate(
            flops=count * 4 * rows * (rows * DK + rows * DV + DK * DV),
            bytes_accessed=count * (rows * 2 * (4 * DK + 4 * DV) + ROWS * DV * 2 * (1 + len(parts))),
            transcendentals=count * 2 * rows * rows,
        ),
        name="span_outputs",
    )(*operands)


def body(
    head_bits,
    ctx_bits,
    query_codes,
    key_codes,
    value_codes,
    block_scales,
    fault_tensor,
    fault_offset,
    fault_bit,
    input_gate,
    forget_gate,
):
    bits = head_bits + ctx_bits
    assert query_codes.shape[0] == CH
    small = (block_scales.transpose(1, 0, 2), fault_tensor, fault_offset, fault_bit)
    codes = (query_codes, key_codes, value_codes)
    exchange = functools.partial(flip, head_bits=head_bits, ctx_bits=ctx_bits)
    run, weight, shift, mf = gates(input_gate.T, forget_gate.T)

    starts = [sum(CHUNKS[:c]) for c in range(len(CHUNKS))]
    assert 2 * sum(CHUNKS) == input_gate.shape[1]
    out = None
    for first, count in zip(starts, CHUNKS):
        keep, send = span_states(first, count, small, mf, weight, key_codes, value_codes)
        got = [exchange(send, 0, last=False)]
        for b in range(1, bits):
            group = combine(head_bits, bits, False, [keep, *got])
            got.append(exchange(group, b, last=b == bits - 1))
        back = exchange(combine(head_bits, bits, True, [keep, *got[1:]]), 0, last=False)
        out = span_outputs(head_bits, bits, first, small, run, shift, codes, back, got, out)
    return out


def solution(mesh):
    rows = P(("grp", "ctx", "head"), None)
    placed = (rows, rows, rows, P(("grp", "ctx", "head"), None, None)) + (rows,) * 5
    return jax.shard_map(
        functools.partial(body, *sizes(mesh)), mesh=mesh, in_specs=placed, out_specs=rows, check_vma=False
    )
```

```python
import functools
import math

import jax
import jax.numpy as jnp
from jax import lax
from jax.experimental import pallas as pl
from jax.experimental.pallas import tpu as pltpu
from jax.sharding import PartitionSpec as P

DK = 256
DV = 512
CH = 256
BLK = 128
NEG_FILL = -1e30
TAIL = 8
ROWS = DK + TAIL
CHUNKS = (1, 1, 1, 1)
AHEAD, DUE, GAP = 2, (8.0, 24.0, 26.5, 34.0, 42.0), 12.0

F32 = jnp.float32
BF16 = jnp.bfloat16


def sizes(mesh):
    ctx, head = mesh.shape["ctx"], mesh.shape["head"]
    head_bits, ctx_bits = head.bit_length() - 1, ctx.bit_length() - 1
    assert head == 1 << head_bits and ctx == 1 << ctx_bits and head_bits >= 1
    return head_bits, ctx_bits


def flip(x, bit, head_bits, ctx_bits, last):
    axis, size, b = (
        ("head", 1 << head_bits, bit) if bit < head_bits else ("ctx", 1 << ctx_bits, bit - head_bits)
    )
    pairs = [(i, i ^ (1 << b)) for i in range(size) if not (last and i & (1 << b))]
    return lax.ppermute(x, axis, pairs)


def gate_kernel(i_ref, f_ref, run_ref, weight_ref, shift_ref, mf_ref):
    gate, x = i_ref[...], f_ref[...].astype(F32)
    log_forget = jnp.minimum(x, 0.0) - jnp.log1p(jnp.exp(-jnp.abs(x)))
    size = x.shape[1]
    row = lax.broadcasted_iota(jnp.int32, (size, size), 0)
    col = lax.broadcasted_iota(jnp.int32, (size, size), 1)
    before = jnp.where(row >= col, 1.0, 0.0).astype(F32)
    same = jnp.where(row == col, 1.0, 0.0).astype(BF16)
    exact = dict(precision=lax.Precision.HIGHEST, preferred_element_type=F32)
    across = (((1,), (1,)), ((), ()))
    running_row = lax.dot_general(log_forget, before, across, **exact)
    running = lax.dot_general(before, log_forget, across, **exact)
    gate_col = lax.dot_general(same, gate, across, preferred_element_type=F32)
    total = running[size - 1 : size, :]
    exponent = total - running + gate_col
    peak = jnp.max(exponent, axis=0, keepdims=True)
    run_ref[...] = running
    weight_ref[...] = jnp.exp(exponent - peak)
    shift_ref[...] = gate.astype(F32) - running_row
    mf_ref[...] = jnp.concatenate([peak, total], axis=0)


def gates(input_gate, forget_gate):
    heads, size = input_gate.shape
    col = jax.ShapeDtypeStruct((size, heads), F32)
    row = jax.ShapeDtypeStruct((heads, size), F32)
    return pl.pallas_call(
        gate_kernel,
        out_shape=(col, col, row, jax.ShapeDtypeStruct((2, heads), F32)),
        compiler_params=pltpu.CompilerParams(vmem_limit_bytes=4 << 20),
        cost_estimate=pl.CostEstimate(flops=1 << 20, bytes_accessed=1 << 20, transcendentals=0),
        name="gates",
    )(input_gate, forget_gate)


def pick(ref, h):
    x = ref[...]
    lane = lax.broadcasted_iota(jnp.int32, x.shape, 1)
    return jnp.sum(jnp.where(lane == h, x, 0.0), axis=1, keepdims=True)


def dequant(ref, at, width, tensor_id, h, scales, tensors, offsets, bits):
    rows = ref.shape[0]
    row = lax.broadcasted_iota(jnp.int32, (BLK, 1), 0)
    col = lax.broadcasted_iota(jnp.int32, (1, width), 1)
    out = []
    for b in range(rows // BLK):
        x = ref[b * BLK : (b + 1) * BLK, pl.ds(at, width)].astype(F32)
        offset, scale = offsets[b, h], scales[tensor_id, b, h]
        hit_row = jnp.where(tensors[b, h] == tensor_id, offset // DV, -1)
        hit_col = (offset % DV) % width
        flipped = -(lax.shift_left(jnp.int32(1), bits[b, h]).astype(F32)) * scale
        out.append((x * jnp.where((row == hit_row) & (col == hit_col), flipped, scale)).astype(BF16))
    return jnp.concatenate(out, axis=0)


def split(x):
    high = x.astype(BF16).astype(F32)
    middle = (x - high).astype(BF16).astype(F32)
    return high, middle, x - high - middle


def pack_tail(normer, peak, total):
    high, middle, least = split(normer)
    rows = [jnp.concatenate([high, middle], axis=1), jnp.concatenate([least, jnp.zeros_like(least)], axis=1)]
    rows += [*split(peak), *split(total)]
    at = lax.broadcasted_iota(jnp.int32, (TAIL, DV), 0)
    out = jnp.zeros((TAIL, DV), F32)
    for r, value in enumerate(rows):
        out = jnp.where(at == r, value, out)
    return out.astype(BF16)


class State:
    def __init__(self, ref, i):
        self.ref, self.i = ref, i
        t = ref[i, DK:ROWS, :].astype(F32)
        self.normer = t[0:1, :DK] + t[0:1, DK : 2 * DK] + t[1:2, :DK]
        self.peak = t[2:3] + t[3:4] + t[4:5]
        self.total = t[5:6] + t[6:7] + t[7:8]

    def matrix(self):
        return self.ref[self.i, :DK, :]


def joined(early, late):
    peak = jnp.maximum(early[0] + late[1], late[0])
    return peak, early[1] + late[1], jnp.exp(early[0] + late[1] - peak), jnp.exp(late[0] - peak)


def group_weights(bit, own, got):
    peak, total, weights = own.peak, own.total, [jnp.ones_like(own.peak)]
    for b, peer in enumerate(got):
        low = joined((peak, total), (peer.peak, peer.total))
        high = joined((peer.peak, peer.total), (peak, total))
        peak, total = jnp.where(bit[b], high[0], low[0]), low[1]
        here, there = jnp.where(bit[b], high[3], low[2]), jnp.where(bit[b], high[2], low[3])
        weights = [w * here for w in weights] + [there]
    return weights, peak, total


def start_weights(bit, include, own, got):
    peak, total, weights = None, None, []
    one = jnp.ones_like(got[-1].peak)
    peak, total = one * NEG_FILL, one * 0.0
    if own is not None:
        peak, total = jnp.where(include, own.peak, peak), jnp.where(include, own.total, total)
        weights = [jnp.where(include, one, 0.0)]
    for b, peer in zip(range(len(bit) - len(got), len(bit)), got):
        new = joined((peer.peak, peer.total), (peak, total))
        weights = [w * jnp.where(bit[b], new[3], 1.0) for w in weights] + [jnp.where(bit[b], new[2], 0.0)]
        peak, total = jnp.where(bit[b], new[0], peak), jnp.where(bit[b], new[1], total)
    return weights, peak, total


def weighted_sum(weights, states):
    matrix, normer = None, None
    for w, state in zip(weights, states):
        term, tail = state.matrix().astype(F32) * w, state.normer * w[:, :DK]
        matrix = term if matrix is None else matrix + term
        normer = tail if normer is None else normer + tail
    return matrix, normer


def device_bits(head_bits, bits):
    me = lax.axis_index("ctx") * (1 << head_bits) + lax.axis_index("head")
    return [((me >> b) & 1) == 1 for b in range(bits)]


def ordered(kernel, operands, after):
    if after is None:
        return kernel, [], []
    at = operands

    def run(*refs):
        kernel(*refs[:at], *refs[at + 1 :])

    return run, [after], [pl.BlockSpec(memory_space=pl.ANY)]


def in_hbm(x):
    return pltpu.with_memory_space_constraint(x, pltpu.HBM)


SMEM = pl.BlockSpec(memory_space=pltpu.SMEM)
VMEM = pl.BlockSpec(memory_space=pltpu.VMEM)


def state_kernel(first, scales, tensors, offsets, fbits, mf, weight_ref, k_ref, v_ref, keep_ref, send_ref):
    own = lax.axis_index("head") & 1
    i = pl.program_id(0)
    for out_ref, side in ((send_ref, 1 - own), (keep_ref, own)):
        h = 2 * (first + i) + side
        info = (h, scales, tensors, offsets, fbits)
        k = dequant(k_ref, pl.multiple_of(side * DK, DK), DK, 1, *info)
        v = dequant(v_ref, pl.multiple_of(side * DV, DV), DV, 2, *info)
        weighted = (k.astype(F32) * pick(weight_ref, h)).astype(BF16)
        matrix = lax.dot_general(weighted, v, (((0,), (0,)), ((), ())), preferred_element_type=F32)
        out_ref[0, :DK, :] = matrix.astype(BF16)
        normer = jnp.sum(weighted.astype(F32), axis=0, keepdims=True)
        out_ref[0, DK:ROWS, :] = pack_tail(normer, jnp.full((1, DV), mf[0, h], F32), jnp.full((1, DV), mf[1, h], F32))


def whole(shape):
    return pl.BlockSpec(shape, lambda i: (0,) * len(shape))


STATE = pl.BlockSpec((1, ROWS, DV), lambda i: (i, 0, 0))


def span_states(first, count, small, mf, weight, key_codes, value_codes, after):
    rows = key_codes.shape[0]
    out = jax.ShapeDtypeStruct((count, ROWS, DV), BF16)
    kernel, extra, extra_specs = ordered(functools.partial(state_kernel, first), 8, after)
    return pl.pallas_call(
        kernel,
        grid=(count,),
        in_specs=[SMEM] * 5
        + [
            whole(weight.shape),
            pl.BlockSpec((rows, 2 * DK), lambda i: (0, first + i)),
            pl.BlockSpec((rows, 2 * DV), lambda i: (0, first + i)),
        ]
        + extra_specs,
        out_specs=(STATE, STATE),
        out_shape=(out, out),
        compiler_params=pltpu.CompilerParams(vmem_limit_bytes=12 << 20),
        cost_estimate=pl.CostEstimate(
            flops=count * 4 * rows * DK * DV, bytes_accessed=count * rows * 2 * (2 * DK + 4 * DV), transcendentals=0
        ),
        name="span_states",
    )(*small, mf, weight, key_codes, value_codes, *extra)


def combine_kernel(head_bits, bits, last, *refs):
    parts, out_ref = refs[:-1], refs[-1]
    bit = device_bits(head_bits, bits)
    for i in range(out_ref.shape[0]):
        states = [State(ref, i) for ref in parts]
        if last:
            weights, peak, total = start_weights(bit, jnp.logical_not(bit[0]), states[0], states[1:])
        else:
            weights, peak, total = group_weights(bit, states[0], states[1:])
        matrix, normer = weighted_sum(weights, states)
        out_ref[i, :DK, :] = matrix.astype(BF16)
        out_ref[i, DK:ROWS, :] = pack_tail(normer, peak, total)


def combine(head_bits, bits, last, parts, after):
    count = parts[0].shape[0]
    kernel, extra, extra_specs = ordered(functools.partial(combine_kernel, head_bits, bits, last), len(parts), after)
    return pl.pallas_call(
        kernel,
        in_specs=[VMEM] * len(parts) + extra_specs,
        out_specs=VMEM,
        out_shape=jax.ShapeDtypeStruct((count, ROWS, DV), BF16),
        compiler_params=pltpu.CompilerParams(vmem_limit_bytes=8 << 20),
        cost_estimate=pl.CostEstimate(
            flops=count * ROWS * DV * 2 * len(parts), bytes_accessed=count * ROWS * DV * 2 * (len(parts) + 1), transcendentals=0
        ),
        name="combine",
    )(*parts, *extra)


def output_kernel(
    head_bits, bits, first, scales, tensors, offsets, fbits, run_ref, shift_ref, q_ref, k_ref, v_ref, back_ref, *rest
):
    parts, out_ref = rest[:bits], rest[-1]
    bit = device_bits(head_bits, bits)
    own = lax.axis_index("head") & 1
    i = pl.program_id(0)
    factor = 1.0 / math.sqrt(DK)
    size = q_ref.shape[0]
    row = lax.broadcasted_iota(jnp.int32, (size, size), 0)
    col = lax.broadcasted_iota(jnp.int32, (size, size), 1)
    for side, mine in ((own, True), (1 - own, False)):
        h = 2 * (first + i) + side
        info = (h, scales, tensors, offsets, fbits)
        if mine:
            states = [State(ref, 0) for ref in parts]
            weights, peak, _ = start_weights(bit, None, None, states)
            start, normer = weighted_sum(weights, states)
            start = start.astype(BF16)
        else:
            back = State(back_ref, 0)
            start, normer, peak = back.matrix(), back.normer, back.peak
        narrow, wide = pl.multiple_of(side * DK, DK), pl.multiple_of(side * DV, DV)
        q = dequant(q_ref, narrow, DK, 0, *info)
        k = dequant(k_ref, narrow, DK, 1, *info)
        v = dequant(v_ref, wide, DV, 2, *info)
        run = pick(run_ref, h)
        exponent = jnp.where(row >= col, run + shift_ref[pl.ds(h, 1), :], NEG_FILL)
        inter = run + peak[:, :1]
        row_peak = jnp.maximum(jnp.max(exponent, axis=1, keepdims=True), inter)
        decay = jnp.exp(exponent - row_peak)
        scores = lax.dot_general(q, k, (((1,), (1,)), ((), ())), preferred_element_type=F32) * factor
        product = decay * scores
        lifted = (q.astype(F32) * (factor * jnp.exp(inter - row_peak))).astype(BF16)
        numerator = jnp.dot(product.astype(BF16), v, preferred_element_type=F32)
        numerator = numerator + jnp.dot(lifted, start, preferred_element_type=F32)
        denominator = jnp.sum(product, axis=1, keepdims=True) + jnp.sum(
            lifted.astype(F32) * normer, axis=1, keepdims=True
        )
        out_ref[:, pl.ds(wide, DV)] = (numerator / jnp.maximum(jnp.abs(denominator), 1.0)).astype(BF16)


def span_outputs(head_bits, bits, first, small, run, shift, codes, back, parts, before, after):
    q, k, v = codes
    count, rows = back.shape[0], q.shape[0]
    narrow = pl.BlockSpec((rows, 2 * DK), lambda i: (0, first + i))
    wide = pl.BlockSpec((rows, 2 * DV), lambda i: (0, first + i))
    operands = [*small, run, shift, q, k, v, back, *parts]
    in_specs = [SMEM] * 4 + [whole(run.shape), whole(shift.shape)] + [narrow, narrow, wide, STATE] + [STATE] * len(parts)
    aliases = {}
    if before is not None:
        aliases = {len(operands): 0}
        operands.append(before)
        in_specs.append(pl.BlockSpec(memory_space=pl.ANY))
    kernel, extra, extra_specs = ordered(functools.partial(output_kernel, head_bits, bits, first), len(operands), after)
    return pl.pallas_call(
        kernel,
        grid=(count,),
        in_specs=in_specs + extra_specs,
        out_specs=wide,
        out_shape=jax.ShapeDtypeStruct(v.shape, BF16),
        input_output_aliases=aliases,
        compiler_params=pltpu.CompilerParams(vmem_limit_bytes=16 << 20),
        cost_estimate=pl.CostEstimate(
            flops=count * 4 * rows * (rows * DK + rows * DV + DK * DV),
            bytes_accessed=count * (rows * 2 * (4 * DK + 4 * DV) + ROWS * DV * 2 * (1 + len(parts))),
            transcendentals=count * 2 * rows * rows,
        ),
        name="span_outputs",
    )(*operands, *extra)


def body(
    head_bits,
    ctx_bits,
    query_codes,
    key_codes,
    value_codes,
    block_scales,
    fault_tensor,
    fault_offset,
    fault_bit,
    input_gate,
    forget_gate,
):
    bits = head_bits + ctx_bits
    assert query_codes.shape[0] == CH
    small = tuple(in_hbm(x) for x in (block_scales.transpose(1, 0, 2), fault_tensor, fault_offset, fault_bit))
    codes = (query_codes, key_codes, value_codes)
    exchange = functools.partial(flip, head_bits=head_bits, ctx_bits=ctx_bits)
    run, weight, shift, mf = gates(in_hbm(input_gate.T), in_hbm(forget_gate.T))

    starts = [sum(CHUNKS[:c]) for c in range(len(CHUNKS))]
    assert 2 * sum(CHUNKS) == input_gate.shape[1]
    keys, values = in_hbm(key_codes), in_hbm(value_codes)
    keep, got, back = {}, {}, {}
    out = token = None
    for stage, c in order(len(CHUNKS), bits):
        first, count = starts[c], CHUNKS[c]
        if stage == 0:
            keep[c], token = span_states(first, count, small, mf, weight, keys, values, token)
        elif stage < bits:
            token = combine(head_bits, bits, False, [keep[c], *got[c]], token)
        elif stage == bits:
            token = combine(head_bits, bits, True, [keep[c], *got[c][1:]], token)
        else:
            out = span_outputs(head_bits, bits, first, small, run, shift, codes, back[c], got[c], out, token)
        if stage < bits:
            got.setdefault(c, []).append(exchange(token, stage, last=stage == bits - 1))
        elif stage == bits:
            back[c] = exchange(token, 0, last=False)
    return out


def order(chunks, bits):
    def due(step):
        stage, c = step
        if stage == 0:
            return 0.1 * c if c < AHEAD else DUE[0] + GAP * (c - AHEAD) + 0.5
        late = bits + 1 - stage
        at = DUE[stage - 1] if stage <= 2 else DUE[4] if late == 0 else DUE[3] if late == 1 else DUE[2] + 0.01 * stage
        return at + GAP * c

    return sorted([(stage, c) for c in range(chunks) for stage in range(bits + 2)], key=due)


def solution(mesh):
    rows = P(("grp", "ctx", "head"), None)
    placed = (rows, rows, rows, P(("grp", "ctx", "head"), None, None)) + (rows,) * 5
    return jax.shard_map(
        functools.partial(body, *sizes(mesh)), mesh=mesh, in_specs=placed, out_specs=rows, check_vma=False
    )
```

```python
import functools
import math

import jax
import jax.numpy as jnp
from jax import lax
from jax.experimental import pallas as pl
from jax.experimental.pallas import tpu as pltpu
from jax.sharding import PartitionSpec as P

DK = 256
DV = 512
CH = 256
BLK = 128
NEG_FILL = -1e30
TAIL = 8
ROWS = DK + TAIL
CHUNKS = ((0, 0, DV), (1, 0, DV), (2, 0, DV), (3, 0, DV))
ORDER = (
    (0, 0), (0, 1), (1, 0), (0, 2), (1, 1), (0, 3), (2, 0), (1, 2), (2, 1), (3, 0), (1, 3), (4, 0),
    (3, 1), (2, 2), (3, 2), (4, 1), (2, 3), (3, 3), (4, 2), (5, 0), (4, 3), (5, 1), (5, 2), (5, 3),
)

F32 = jnp.float32
BF16 = jnp.bfloat16


def sizes(mesh):
    ctx, head = mesh.shape["ctx"], mesh.shape["head"]
    head_bits, ctx_bits = head.bit_length() - 1, ctx.bit_length() - 1
    assert head == 1 << head_bits and ctx == 1 << ctx_bits and head_bits >= 1
    return head_bits, ctx_bits


def flip(x, bit, head_bits, ctx_bits, last):
    axis, size, b = (
        ("head", 1 << head_bits, bit) if bit < head_bits else ("ctx", 1 << ctx_bits, bit - head_bits)
    )
    pairs = [(i, i ^ (1 << b)) for i in range(size) if not (last and i & (1 << b))]
    return lax.ppermute(x, axis, pairs)


def gate_kernel(i_ref, f_ref, run_ref, weight_ref, shift_ref, mf_ref):
    gate, x = i_ref[...], f_ref[...].astype(F32)
    log_forget = jnp.minimum(x, 0.0) - jnp.log1p(jnp.exp(-jnp.abs(x)))
    size = x.shape[1]
    row = lax.broadcasted_iota(jnp.int32, (size, size), 0)
    col = lax.broadcasted_iota(jnp.int32, (size, size), 1)
    before = jnp.where(row >= col, 1.0, 0.0).astype(F32)
    same = jnp.where(row == col, 1.0, 0.0).astype(BF16)
    exact = dict(precision=lax.Precision.HIGHEST, preferred_element_type=F32)
    across = (((1,), (1,)), ((), ()))
    running_row = lax.dot_general(log_forget, before, across, **exact)
    running = lax.dot_general(before, log_forget, across, **exact)
    gate_col = lax.dot_general(same, gate, across, preferred_element_type=F32)
    total = running[size - 1 : size, :]
    exponent = total - running + gate_col
    peak = jnp.max(exponent, axis=0, keepdims=True)
    run_ref[...] = running
    weight_ref[...] = jnp.exp(exponent - peak)
    shift_ref[...] = gate.astype(F32) - running_row
    mf_ref[...] = jnp.concatenate([peak, total], axis=0)


def gates(input_gate, forget_gate):
    heads, size = input_gate.shape
    col = jax.ShapeDtypeStruct((size, heads), F32)
    row = jax.ShapeDtypeStruct((heads, size), F32)
    return pl.pallas_call(
        gate_kernel,
        out_shape=(col, col, row, jax.ShapeDtypeStruct((2, heads), F32)),
        compiler_params=pltpu.CompilerParams(vmem_limit_bytes=4 << 20),
        cost_estimate=pl.CostEstimate(flops=1 << 20, bytes_accessed=1 << 20, transcendentals=0),
        name="gates",
    )(input_gate, forget_gate)


def pick(ref, h):
    x = ref[...]
    lane = lax.broadcasted_iota(jnp.int32, x.shape, 1)
    return jnp.sum(jnp.where(lane == h, x, 0.0), axis=1, keepdims=True)


def dequant(ref, at, lo, width, full, tensor_id, h, scales, tensors, offsets, bits):
    rows = ref.shape[0]
    row = lax.broadcasted_iota(jnp.int32, (BLK, 1), 0)
    col = lax.broadcasted_iota(jnp.int32, (1, width), 1) + lo
    out = []
    for b in range(rows // BLK):
        x = ref[b * BLK : (b + 1) * BLK, pl.ds(pl.multiple_of(at + lo, 128), width)].astype(F32)
        offset, scale = offsets[b, h], scales[tensor_id, b, h]
        hit_row = jnp.where(tensors[b, h] == tensor_id, offset // DV, -1)
        hit_col = (offset % DV) % full
        flipped = -(lax.shift_left(jnp.int32(1), bits[b, h]).astype(F32)) * scale
        out.append((x * jnp.where((row == hit_row) & (col == hit_col), flipped, scale)).astype(BF16))
    return jnp.concatenate(out, axis=0)


def split(x):
    high = x.astype(BF16).astype(F32)
    middle = (x - high).astype(BF16).astype(F32)
    return high, middle, x - high - middle


def pack_tail(normer, peak, total):
    width = peak.shape[1]
    blank = jnp.zeros((1, width - DK), F32)
    rows = [jnp.concatenate([x, blank], axis=1) if width > DK else x for x in split(normer)[:2]]
    rows += [*split(peak), *split(total)]
    at = lax.broadcasted_iota(jnp.int32, (TAIL, width), 0)
    out = jnp.zeros((TAIL, width), F32)
    for r, value in enumerate(rows):
        out = jnp.where(at == r, value, out)
    return out.astype(BF16)


class State:
    def __init__(self, ref):
        self.ref = ref
        t = ref[DK:ROWS, :].astype(F32)
        self.normer = t[0:1, :DK] + t[1:2, :DK]
        self.peak = t[2:3] + t[3:4] + t[4:5]
        self.total = t[5:6] + t[6:7] + t[7:8]

    def matrix(self):
        return self.ref[:DK, :]


def joined(early, late):
    peak = jnp.maximum(early[0] + late[1], late[0])
    return peak, early[1] + late[1], jnp.exp(early[0] + late[1] - peak), jnp.exp(late[0] - peak)


def group_weights(bit, own, got):
    peak, total, weights = own.peak, own.total, [jnp.ones_like(own.peak)]
    for b, peer in enumerate(got):
        low = joined((peak, total), (peer.peak, peer.total))
        high = joined((peer.peak, peer.total), (peak, total))
        peak, total = jnp.where(bit[b], high[0], low[0]), low[1]
        here, there = jnp.where(bit[b], high[3], low[2]), jnp.where(bit[b], high[2], low[3])
        weights = [w * here for w in weights] + [there]
    return weights, peak, total


def start_weights(bit, include, own, got):
    peak, total, weights = None, None, []
    one = jnp.ones_like(got[-1].peak)
    peak, total = one * NEG_FILL, one * 0.0
    if own is not None:
        peak, total = jnp.where(include, own.peak, peak), jnp.where(include, own.total, total)
        weights = [jnp.where(include, one, 0.0)]
    for b, peer in zip(range(len(bit) - len(got), len(bit)), got):
        new = joined((peer.peak, peer.total), (peak, total))
        weights = [w * jnp.where(bit[b], new[3], 1.0) for w in weights] + [jnp.where(bit[b], new[2], 0.0)]
        peak, total = jnp.where(bit[b], new[0], peak), jnp.where(bit[b], new[1], total)
    return weights, peak, total


def weighted_sum(weights, states):
    matrix, normer = None, None
    for w, state in zip(weights, states):
        term, tail = state.matrix().astype(F32) * w, state.normer * w[:, :DK]
        matrix = term if matrix is None else matrix + term
        normer = tail if normer is None else normer + tail
    return matrix, normer


def device_bits(head_bits, bits):
    me = lax.axis_index("ctx") * (1 << head_bits) + lax.axis_index("head")
    return [((me >> b) & 1) == 1 for b in range(bits)]


def ordered(kernel, operands, after):
    if after is None:
        return kernel, [], []
    at = operands

    def run(*refs):
        kernel(*refs[:at], *refs[at + 1 :])

    return run, [after], [pl.BlockSpec(memory_space=pl.ANY)]


def in_hbm(x):
    return pltpu.with_memory_space_constraint(x, pltpu.HBM)


SMEM = pl.BlockSpec(memory_space=pltpu.SMEM)
VMEM = pl.BlockSpec(memory_space=pltpu.VMEM)


def state_kernel(pair, lo, scales, tensors, offsets, fbits, mf, weight_ref, k_ref, v_ref, keep_ref, send_ref):
    own = lax.axis_index("head") & 1
    width = keep_ref.shape[1]
    for out_ref, side in ((send_ref, 1 - own), (keep_ref, own)):
        h = 2 * pair + side
        info = (h, scales, tensors, offsets, fbits)
        k = dequant(k_ref, pl.multiple_of(side * DK, DK), 0, DK, DK, 1, *info)
        v = dequant(v_ref, pl.multiple_of(side * DV, DV), lo, width, DV, 2, *info)
        weighted = (k.astype(F32) * pick(weight_ref, h)).astype(BF16)
        matrix = lax.dot_general(weighted, v, (((0,), (0,)), ((), ())), preferred_element_type=F32)
        out_ref[:DK, :] = matrix.astype(BF16)
        normer = jnp.sum(weighted.astype(F32), axis=0, keepdims=True)
        peak, total = jnp.full((1, width), mf[0, h], F32), jnp.full((1, width), mf[1, h], F32)
        out_ref[DK:ROWS, :] = pack_tail(normer, peak, total)


def whole(shape):
    return pl.BlockSpec(shape, lambda i: (0,) * len(shape))


def span_states(chunk, small, mf, weight, key_codes, value_codes, after):
    pair, lo, width = chunk
    rows = key_codes.shape[0]
    out = jax.ShapeDtypeStruct((ROWS, width), BF16)
    kernel, extra, extra_specs = ordered(functools.partial(state_kernel, pair, lo), 8, after)
    return pl.pallas_call(
        kernel,
        grid=(1,),
        in_specs=[SMEM] * 5
        + [
            whole(weight.shape),
            pl.BlockSpec((rows, 2 * DK), lambda i: (0, pair)),
            pl.BlockSpec((rows, 2 * DV), lambda i: (0, pair)),
        ]
        + extra_specs,
        out_specs=(whole(out.shape),) * 2,
        out_shape=(out, out),
        compiler_params=pltpu.CompilerParams(vmem_limit_bytes=12 << 20),
        cost_estimate=pl.CostEstimate(
            flops=4 * rows * DK * width, bytes_accessed=rows * 2 * (2 * DK + 4 * DV), transcendentals=0
        ),
        name="span_states",
    )(*small, mf, weight, key_codes, value_codes, *extra)


def combine_kernel(head_bits, bits, last, *refs):
    parts, out_ref = refs[:-1], refs[-1]
    bit = device_bits(head_bits, bits)
    states = [State(ref) for ref in parts]
    if last:
        weights, peak, total = start_weights(bit, jnp.logical_not(bit[0]), states[0], states[1:])
    else:
        weights, peak, total = group_weights(bit, states[0], states[1:])
    matrix, normer = weighted_sum(weights, states)
    out_ref[:DK, :] = matrix.astype(BF16)
    out_ref[DK:ROWS, :] = pack_tail(normer, peak, total)


def combine(head_bits, bits, last, parts, after):
    size = parts[0].size
    kernel, extra, extra_specs = ordered(functools.partial(combine_kernel, head_bits, bits, last), len(parts), after)
    return pl.pallas_call(
        kernel,
        in_specs=[VMEM] * len(parts) + extra_specs,
        out_specs=VMEM,
        out_shape=jax.ShapeDtypeStruct(parts[0].shape, BF16),
        compiler_params=pltpu.CompilerParams(vmem_limit_bytes=8 << 20),
        cost_estimate=pl.CostEstimate(
            flops=size * 2 * len(parts), bytes_accessed=size * 2 * (len(parts) + 1), transcendentals=0
        ),
        name="combine",
    )(*parts, *extra)


def output_kernel(
    head_bits, bits, pair, pieces, scales, tensors, offsets, fbits, run_ref, shift_ref, q_ref, k_ref, v_ref, *rest
):
    groups = [rest[p * (bits + 1) : (p + 1) * (bits + 1)] for p in range(pieces)]
    out_ref, token_ref = rest[-2:]
    token_ref[...] = jnp.zeros_like(token_ref)
    bit = device_bits(head_bits, bits)
    own = lax.axis_index("head") & 1
    factor = 1.0 / math.sqrt(DK)
    size = q_ref.shape[0]
    row = lax.broadcasted_iota(jnp.int32, (size, size), 0)
    col = lax.broadcasted_iota(jnp.int32, (size, size), 1)
    for side, mine in ((own, True), (1 - own, False)):
        h = 2 * pair + side
        info = (h, scales, tensors, offsets, fbits)
        starts = []
        for back_ref, *parts in groups:
            if mine:
                states = [State(ref) for ref in parts]
                weights, peak, _ = start_weights(bit, None, None, states)
                start, normer = weighted_sum(weights, states)
                starts.append(start.astype(BF16))
            else:
                back = State(back_ref)
                normer, peak = back.normer, back.peak
                starts.append(back.matrix())
        start = jnp.concatenate(starts, axis=1) if pieces > 1 else starts[0]
        narrow, wide = pl.multiple_of(side * DK, DK), pl.multiple_of(side * DV, DV)
        q = dequant(q_ref, narrow, 0, DK, DK, 0, *info)
        k = dequant(k_ref, narrow, 0, DK, DK, 1, *info)
        v = dequant(v_ref, wide, 0, DV, DV, 2, *info)
        run = pick(run_ref, h)
        exponent = jnp.where(row >= col, run + shift_ref[pl.ds(h, 1), :], NEG_FILL)
        inter = run + peak[:, :1]
        row_peak = jnp.maximum(jnp.max(exponent, axis=1, keepdims=True), inter)
        decay = jnp.exp(exponent - row_peak)
        scores = lax.dot_general(q, k, (((1,), (1,)), ((), ())), preferred_element_type=F32) * factor
        product = decay * scores
        lifted = (q.astype(F32) * (factor * jnp.exp(inter - row_peak))).astype(BF16)
        numerator = jnp.dot(product.astype(BF16), v, preferred_element_type=F32)
        numerator = numerator + jnp.dot(lifted, start, preferred_element_type=F32)
        denominator = jnp.sum(product, axis=1, keepdims=True) + jnp.sum(
            lifted.astype(F32) * normer, axis=1, keepdims=True
        )
        out_ref[:, pl.ds(wide, DV)] = (numerator / jnp.maximum(jnp.abs(denominator), 1.0)).astype(BF16)


def span_outputs(head_bits, bits, pair, small, run, shift, codes, groups, before, after):
    q, k, v = codes
    rows = q.shape[0]
    narrow = pl.BlockSpec((rows, 2 * DK), lambda i: (0, pair))
    wide = pl.BlockSpec((rows, 2 * DV), lambda i: (0, pair))
    states = [x for group in groups for x in group]
    operands = [*small, run, shift, q, k, v, *states]
    in_specs = [SMEM] * 4 + [whole(run.shape), whole(shift.shape), narrow, narrow, wide]
    in_specs += [whole(x.shape) for x in states]
    aliases = {}
    if before is not None:
        aliases = {len(operands): 0}
        operands.append(before)
        in_specs.append(pl.BlockSpec(memory_space=pl.ANY))
    kernel, extra, extra_specs = ordered(
        functools.partial(output_kernel, head_bits, bits, pair, len(groups)), len(operands), after
    )
    return pl.pallas_call(
        kernel,
        grid=(1,),
        in_specs=in_specs + extra_specs,
        out_specs=(wide, whole((8, 128))),
        out_shape=(jax.ShapeDtypeStruct(v.shape, BF16), jax.ShapeDtypeStruct((8, 128), F32)),
        input_output_aliases=aliases,
        compiler_params=pltpu.CompilerParams(vmem_limit_bytes=16 << 20),
        cost_estimate=pl.CostEstimate(
            flops=4 * rows * (rows * DK + rows * DV + DK * DV),
            bytes_accessed=rows * 2 * (4 * DK + 4 * DV) + sum(x.size for x in states) * 2,
            transcendentals=2 * rows * rows,
        ),
        name="span_outputs",
    )(*operands, *extra)


def body(
    head_bits,
    ctx_bits,
    query_codes,
    key_codes,
    value_codes,
    block_scales,
    fault_tensor,
    fault_offset,
    fault_bit,
    input_gate,
    forget_gate,
):
    bits = head_bits + ctx_bits
    assert query_codes.shape[0] == CH
    assert sum(width for _, _, width in CHUNKS) * 2 == value_codes.shape[1]
    small = tuple(in_hbm(x) for x in (block_scales.transpose(1, 0, 2), fault_tensor, fault_offset, fault_bit))
    codes = (query_codes, key_codes, value_codes)
    exchange = functools.partial(flip, head_bits=head_bits, ctx_bits=ctx_bits)
    run, weight, shift, mf = gates(in_hbm(input_gate.T), in_hbm(forget_gate.T))
    keys, values = in_hbm(key_codes), in_hbm(value_codes)
    keep, got, back = {}, {}, {}
    out = token = None
    for stage, c in order(bits):
        if stage == 0:
            keep[c], token = span_states(CHUNKS[c], small, mf, weight, keys, values, token)
        elif stage < bits:
            token = combine(head_bits, bits, False, [keep[c], *got[c]], token)
        elif stage == bits:
            token = combine(head_bits, bits, True, [keep[c], *got[c][1:]], token)
        else:
            groups = [[back[d], *got[d]] for d in of_pair(c)]
            out, token = span_outputs(head_bits, bits, c, small, run, shift, codes, groups, out, token)
        if stage < bits:
            got.setdefault(c, []).append(exchange(token, stage, last=stage == bits - 1))
        elif stage == bits:
            back[c] = exchange(token, 0, last=False)
    return out


def of_pair(pair):
    return [c for c, chunk in enumerate(CHUNKS) if chunk[0] == pair]


def order(bits):
    stages = {0: [0], 1: [1], 2: range(2, bits - 1), 3: [bits - 1], 4: [bits], 5: [bits + 1]}
    return [(stage, c) for place, c in ORDER for stage in stages[place]]


def solution(mesh):
    rows = P(("grp", "ctx", "head"), None)
    placed = (rows, rows, rows, P(("grp", "ctx", "head"), None, None)) + (rows,) * 5
    return jax.shard_map(
        functools.partial(body, *sizes(mesh)), mesh=mesh, in_specs=placed, out_specs=rows, check_vma=False
    )
```

```python
import functools
import math

import jax
import jax.numpy as jnp
from jax import lax
from jax.experimental import pallas as pl
from jax.experimental.pallas import tpu as pltpu
from jax.sharding import PartitionSpec as P

DK = 256
DV = 512
CH = 256
BLK = 128
NEG_FILL = -1e30
TAIL = 8
ROWS = DK + TAIL
CHUNKS = ((0, 0, DV // 2), (0, DV // 2, DV // 2), (1, 0, DV), (2, 0, DV), (3, 0, DV))
ORDER = (
    (0, 0), (0, 1), (0, 2), (1, 0), (1, 1), (0, 3), (1, 2), (2, 1), (0, 4), (1, 3), (2, 0), (3, 0), (3, 1), (2, 2),
    (4, 0), (1, 4), (3, 2), (4, 1), (5, 0), (2, 3), (3, 3), (5, 1), (4, 2), (2, 4), (3, 4), (4, 3), (6, 0), (6, 1),
    (4, 4), (5, 3), (6, 2), (5, 2), (6, 3),
)

F32 = jnp.float32
BF16 = jnp.bfloat16


def sizes(mesh):
    ctx, head = mesh.shape["ctx"], mesh.shape["head"]
    head_bits, ctx_bits = head.bit_length() - 1, ctx.bit_length() - 1
    assert head == 1 << head_bits and ctx == 1 << ctx_bits and head_bits >= 1
    return head_bits, ctx_bits


def flip(x, bit, head_bits, ctx_bits, last):
    axis, size, b = (
        ("head", 1 << head_bits, bit) if bit < head_bits else ("ctx", 1 << ctx_bits, bit - head_bits)
    )
    pairs = [(i, i ^ (1 << b)) for i in range(size) if not (last and i & (1 << b))]
    return lax.ppermute(x, axis, pairs)


def gate_kernel(i_ref, f_ref, run_ref, weight_ref, shift_ref, mf_ref):
    gate, x = i_ref[...], f_ref[...].astype(F32)
    log_forget = jnp.minimum(x, 0.0) - jnp.log1p(jnp.exp(-jnp.abs(x)))
    size = x.shape[1]
    row = lax.broadcasted_iota(jnp.int32, (size, size), 0)
    col = lax.broadcasted_iota(jnp.int32, (size, size), 1)
    before = jnp.where(row >= col, 1.0, 0.0).astype(F32)
    same = jnp.where(row == col, 1.0, 0.0).astype(BF16)
    exact = dict(precision=lax.Precision.HIGHEST, preferred_element_type=F32)
    across = (((1,), (1,)), ((), ()))
    running_row = lax.dot_general(log_forget, before, across, **exact)
    running = lax.dot_general(before, log_forget, across, **exact)
    gate_col = lax.dot_general(same, gate, across, preferred_element_type=F32)
    total = running[size - 1 : size, :]
    exponent = total - running + gate_col
    peak = jnp.max(exponent, axis=0, keepdims=True)
    run_ref[...] = running
    weight_ref[...] = jnp.exp(exponent - peak)
    shift_ref[...] = gate.astype(F32) - running_row
    mf_ref[...] = jnp.concatenate([peak, total], axis=0)


def gates(input_gate, forget_gate):
    heads, size = input_gate.shape
    col = jax.ShapeDtypeStruct((size, heads), F32)
    row = jax.ShapeDtypeStruct((heads, size), F32)
    return pl.pallas_call(
        gate_kernel,
        out_shape=(col, col, row, jax.ShapeDtypeStruct((2, heads), F32)),
        compiler_params=pltpu.CompilerParams(vmem_limit_bytes=4 << 20),
        cost_estimate=pl.CostEstimate(flops=1 << 20, bytes_accessed=1 << 20, transcendentals=0),
        name="gates",
    )(input_gate, forget_gate)


def pick(ref, h):
    x = ref[...]
    lane = lax.broadcasted_iota(jnp.int32, x.shape, 1)
    return jnp.sum(jnp.where(lane == h, x, 0.0), axis=1, keepdims=True)


def dequant(ref, at, lo, width, full, tensor_id, h, scales, tensors, offsets, bits):
    rows = ref.shape[0]
    row = lax.broadcasted_iota(jnp.int32, (BLK, 1), 0)
    col = lax.broadcasted_iota(jnp.int32, (1, width), 1) + lo
    out = []
    for b in range(rows // BLK):
        x = ref[b * BLK : (b + 1) * BLK, pl.ds(pl.multiple_of(at + lo, 128), width)].astype(F32)
        offset, scale = offsets[b, h], scales[tensor_id, b, h]
        hit_row = jnp.where(tensors[b, h] == tensor_id, offset // DV, -1)
        hit_col = (offset % DV) % full
        flipped = -(lax.shift_left(jnp.int32(1), bits[b, h]).astype(F32)) * scale
        out.append((x * jnp.where((row == hit_row) & (col == hit_col), flipped, scale)).astype(BF16))
    return jnp.concatenate(out, axis=0)


def split(x):
    high = x.astype(BF16).astype(F32)
    middle = (x - high).astype(BF16).astype(F32)
    return high, middle, x - high - middle


def pack_tail(normer, peak, total):
    width = peak.shape[1]
    blank = jnp.zeros((1, width - DK), F32)
    rows = [jnp.concatenate([x, blank], axis=1) if width > DK else x for x in split(normer)[:2]]
    rows += [*split(peak), *split(total)]
    at = lax.broadcasted_iota(jnp.int32, (TAIL, width), 0)
    out = jnp.zeros((TAIL, width), F32)
    for r, value in enumerate(rows):
        out = jnp.where(at == r, value, out)
    return out.astype(BF16)


class State:
    def __init__(self, ref):
        self.ref = ref
        t = ref[DK:ROWS, :].astype(F32)
        self.normer = t[0:1, :DK] + t[1:2, :DK]
        self.peak = t[2:3] + t[3:4] + t[4:5]
        self.total = t[5:6] + t[6:7] + t[7:8]

    def matrix(self):
        return self.ref[:DK, :]


def joined(early, late):
    peak = jnp.maximum(early[0] + late[1], late[0])
    return peak, early[1] + late[1], jnp.exp(early[0] + late[1] - peak), jnp.exp(late[0] - peak)


def group_weights(bit, own, got):
    peak, total, weights = own.peak, own.total, [jnp.ones_like(own.peak)]
    for b, peer in enumerate(got):
        low = joined((peak, total), (peer.peak, peer.total))
        high = joined((peer.peak, peer.total), (peak, total))
        peak, total = jnp.where(bit[b], high[0], low[0]), low[1]
        here, there = jnp.where(bit[b], high[3], low[2]), jnp.where(bit[b], high[2], low[3])
        weights = [w * here for w in weights] + [there]
    return weights, peak, total


def start_weights(bit, include, own, got):
    peak, total, weights = None, None, []
    one = jnp.ones_like(got[-1].peak)
    peak, total = one * NEG_FILL, one * 0.0
    if own is not None:
        peak, total = jnp.where(include, own.peak, peak), jnp.where(include, own.total, total)
        weights = [jnp.where(include, one, 0.0)]
    for b, peer in zip(range(len(bit) - len(got), len(bit)), got):
        new = joined((peer.peak, peer.total), (peak, total))
        weights = [w * jnp.where(bit[b], new[3], 1.0) for w in weights] + [jnp.where(bit[b], new[2], 0.0)]
        peak, total = jnp.where(bit[b], new[0], peak), jnp.where(bit[b], new[1], total)
    return weights, peak, total


def weighted_sum(weights, states):
    matrix, normer = None, None
    for w, state in zip(weights, states):
        term, tail = state.matrix().astype(F32) * w, state.normer * w[:, :DK]
        matrix = term if matrix is None else matrix + term
        normer = tail if normer is None else normer + tail
    return matrix, normer


def device_bits(head_bits, bits):
    me = lax.axis_index("ctx") * (1 << head_bits) + lax.axis_index("head")
    return [((me >> b) & 1) == 1 for b in range(bits)]


def ordered(kernel, operands, after):
    if after is None:
        return kernel, [], []
    at = operands

    def run(*refs):
        kernel(*refs[:at], *refs[at + 1 :])

    return run, [after], [pl.BlockSpec(memory_space=pl.ANY)]


def in_hbm(x):
    return pltpu.with_memory_space_constraint(x, pltpu.HBM)


SMEM = pl.BlockSpec(memory_space=pltpu.SMEM)
VMEM = pl.BlockSpec(memory_space=pltpu.VMEM)


def state_kernel(pair, lo, scales, tensors, offsets, fbits, mf, weight_ref, k_ref, v_ref, keep_ref, send_ref):
    own = lax.axis_index("head") & 1
    width = keep_ref.shape[1]
    for out_ref, side in ((send_ref, 1 - own), (keep_ref, own)):
        h = 2 * pair + side
        info = (h, scales, tensors, offsets, fbits)
        k = dequant(k_ref, pl.multiple_of(side * DK, DK), 0, DK, DK, 1, *info)
        v = dequant(v_ref, pl.multiple_of(side * DV, DV), lo, width, DV, 2, *info)
        weighted = (k.astype(F32) * pick(weight_ref, h)).astype(BF16)
        matrix = lax.dot_general(weighted, v, (((0,), (0,)), ((), ())), preferred_element_type=F32)
        out_ref[:DK, :] = matrix.astype(BF16)
        normer = jnp.sum(weighted.astype(F32), axis=0, keepdims=True)
        peak, total = jnp.full((1, width), mf[0, h], F32), jnp.full((1, width), mf[1, h], F32)
        out_ref[DK:ROWS, :] = pack_tail(normer, peak, total)


def whole(shape):
    return pl.BlockSpec(shape, lambda i: (0,) * len(shape))


def span_states(chunk, small, mf, weight, key_codes, value_codes, after):
    pair, lo, width = chunk
    rows = key_codes.shape[0]
    out = jax.ShapeDtypeStruct((ROWS, width), BF16)
    kernel, extra, extra_specs = ordered(functools.partial(state_kernel, pair, lo), 8, after)
    return pl.pallas_call(
        kernel,
        grid=(1,),
        in_specs=[SMEM] * 5
        + [
            whole(weight.shape),
            pl.BlockSpec((rows, 2 * DK), lambda i: (0, pair)),
            pl.BlockSpec((rows, 2 * DV), lambda i: (0, pair)),
        ]
        + extra_specs,
        out_specs=(whole(out.shape),) * 2,
        out_shape=(out, out),
        compiler_params=pltpu.CompilerParams(vmem_limit_bytes=12 << 20),
        cost_estimate=pl.CostEstimate(
            flops=4 * rows * DK * width, bytes_accessed=rows * 2 * (2 * DK + 4 * DV), transcendentals=0
        ),
        name="span_states",
    )(*small, mf, weight, key_codes, value_codes, *extra)


def combine_kernel(head_bits, bits, last, *refs):
    parts, out_ref = refs[:-1], refs[-1]
    bit = device_bits(head_bits, bits)
    states = [State(ref) for ref in parts]
    if last:
        weights, peak, total = start_weights(bit, jnp.logical_not(bit[0]), states[0], states[1:])
    else:
        weights, peak, total = group_weights(bit, states[0], states[1:])
    matrix, normer = weighted_sum(weights, states)
    out_ref[:DK, :] = matrix.astype(BF16)
    out_ref[DK:ROWS, :] = pack_tail(normer, peak, total)


def combine(head_bits, bits, last, parts, after):
    size = parts[0].size
    kernel, extra, extra_specs = ordered(functools.partial(combine_kernel, head_bits, bits, last), len(parts), after)
    return pl.pallas_call(
        kernel,
        in_specs=[VMEM] * len(parts) + extra_specs,
        out_specs=VMEM,
        out_shape=jax.ShapeDtypeStruct(parts[0].shape, BF16),
        compiler_params=pltpu.CompilerParams(vmem_limit_bytes=8 << 20),
        cost_estimate=pl.CostEstimate(
            flops=size * 2 * len(parts), bytes_accessed=size * 2 * (len(parts) + 1), transcendentals=0
        ),
        name="combine",
    )(*parts, *extra)


def output_kernel(
    head_bits, bits, pair, mine, pieces, scales, tensors, offsets, fbits, run_ref, shift_ref, q_ref, k_ref, v_ref, *rest
):
    count = len(rest[:-2]) // pieces
    groups = [rest[p * count : (p + 1) * count] for p in range(pieces)]
    out_ref, token_ref = rest[-2:]
    token_ref[...] = jnp.zeros_like(token_ref)
    bit = device_bits(head_bits, bits)
    h = 2 * pair + head_side(mine)
    factor = 1.0 / math.sqrt(DK)
    size = q_ref.shape[0]
    row = lax.broadcasted_iota(jnp.int32, (size, size), 0)
    col = lax.broadcasted_iota(jnp.int32, (size, size), 1)
    info = (h, scales, tensors, offsets, fbits)
    starts = []
    for group in groups:
        states = [State(ref) for ref in group]
        if mine:
            weights, peak, _ = start_weights(bit, None, None, states)
            start, normer = weighted_sum(weights, states)
            starts.append(start.astype(BF16))
        else:
            normer, peak = states[0].normer, states[0].peak
            starts.append(states[0].matrix())
    start = jnp.concatenate(starts, axis=1) if pieces > 1 else starts[0]
    q = dequant(q_ref, 0, 0, DK, DK, 0, *info)
    k = dequant(k_ref, 0, 0, DK, DK, 1, *info)
    v = dequant(v_ref, 0, 0, DV, DV, 2, *info)
    run = pick(run_ref, h)
    exponent = jnp.where(row >= col, run + shift_ref[pl.ds(h, 1), :], NEG_FILL)
    inter = run + peak[:, :1]
    row_peak = jnp.maximum(jnp.max(exponent, axis=1, keepdims=True), inter)
    decay = jnp.exp(exponent - row_peak)
    scores = lax.dot_general(q, k, (((1,), (1,)), ((), ())), preferred_element_type=F32) * factor
    product = decay * scores
    lifted = (q.astype(F32) * (factor * jnp.exp(inter - row_peak))).astype(BF16)
    numerator = jnp.dot(product.astype(BF16), v, preferred_element_type=F32)
    numerator = numerator + jnp.dot(lifted, start, preferred_element_type=F32)
    denominator = jnp.sum(product, axis=1, keepdims=True) + jnp.sum(lifted.astype(F32) * normer, axis=1, keepdims=True)
    out_ref[...] = (numerator / jnp.maximum(jnp.abs(denominator), 1.0)).astype(BF16)


def head_side(mine):
    own = lax.axis_index("head") & 1
    return own if mine else 1 - own


def span_outputs(head_bits, bits, pair, mine, small, run, shift, codes, groups, before, after):
    q, k, v = codes
    rows = q.shape[0]
    narrow = pl.BlockSpec((rows, DK), lambda i: (0, 2 * pair + head_side(mine)))
    wide = pl.BlockSpec((rows, DV), lambda i: (0, 2 * pair + head_side(mine)))
    states = [x for group in groups for x in group]
    operands = [*small, run, shift, q, k, v, *states]
    in_specs = [SMEM] * 4 + [whole(run.shape), whole(shift.shape), narrow, narrow, wide]
    in_specs += [whole(x.shape) for x in states]
    kernel = functools.partial(output_kernel, head_bits, bits, pair, mine, len(groups))
    kernel, extra, extra_specs = ordered(kernel, len(operands), after)
    operands += extra
    in_specs += extra_specs
    aliases = {}
    if before is not None:
        kernel, extra, extra_specs = ordered(kernel, len(operands), before)
        aliases = {len(operands): 0}
        operands += extra
        in_specs += extra_specs
    return pl.pallas_call(
        kernel,
        grid=(1,),
        in_specs=in_specs,
        out_specs=(wide, whole((8, 128))),
        out_shape=(jax.ShapeDtypeStruct(v.shape, BF16), jax.ShapeDtypeStruct((8, 128), F32)),
        input_output_aliases=aliases,
        compiler_params=pltpu.CompilerParams(vmem_limit_bytes=16 << 20),
        cost_estimate=pl.CostEstimate(
            flops=2 * rows * (rows * DK + rows * DV + DK * DV),
            bytes_accessed=rows * 2 * (2 * DK + 2 * DV) + sum(x.size for x in states) * 2,
            transcendentals=rows * rows,
        ),
        name="span_outputs",
    )(*operands)


def body(
    head_bits,
    ctx_bits,
    query_codes,
    key_codes,
    value_codes,
    block_scales,
    fault_tensor,
    fault_offset,
    fault_bit,
    input_gate,
    forget_gate,
):
    bits = head_bits + ctx_bits
    assert query_codes.shape[0] == CH
    assert sum(width for _, _, width in CHUNKS) * 2 == value_codes.shape[1]
    small = tuple(in_hbm(x) for x in (block_scales.transpose(1, 0, 2), fault_tensor, fault_offset, fault_bit))
    codes = (query_codes, key_codes, value_codes)
    exchange = functools.partial(flip, head_bits=head_bits, ctx_bits=ctx_bits)
    run, weight, shift, mf = gates(in_hbm(input_gate.T), in_hbm(forget_gate.T))
    keys, values = in_hbm(key_codes), in_hbm(value_codes)
    keep, got, back = {}, {}, {}
    out = token = None
    for stage, c in order(bits):
        if stage == 0:
            keep[c], token = span_states(CHUNKS[c], small, mf, weight, keys, values, token)
        elif stage < bits:
            token = combine(head_bits, bits, False, [keep[c], *got[c]], token)
        elif stage == bits:
            token = combine(head_bits, bits, True, [keep[c], *got[c][1:]], token)
        else:
            mine = stage == bits + 1
            groups = [got[d] if mine else [back[d]] for d in of_pair(c)]
            out, token = span_outputs(
                head_bits, bits, c, mine, small, run, shift, codes, groups, out, token
            )
        if stage < bits:
            got.setdefault(c, []).append(exchange(token, stage, last=stage == bits - 1))
        elif stage == bits:
            back[c] = exchange(token, 0, last=False)
    return out


def of_pair(pair):
    return [c for c, chunk in enumerate(CHUNKS) if chunk[0] == pair]


def order(bits):
    stages = {0: [0], 1: [1], 2: range(2, bits - 1), 3: [bits - 1], 4: [bits], 5: [bits + 1], 6: [bits + 2]}
    return [(stage, c) for place, c in ORDER for stage in stages[place]]


def solution(mesh):
    rows = P(("grp", "ctx", "head"), None)
    placed = (rows, rows, rows, P(("grp", "ctx", "head"), None, None)) + (rows,) * 5
    return jax.shard_map(
        functools.partial(body, *sizes(mesh)), mesh=mesh, in_specs=placed, out_specs=rows, check_vma=False
    )
```

```python
import functools
import math

import jax
import jax.numpy as jnp
from jax import lax
from jax.experimental import pallas as pl
from jax.experimental.pallas import tpu as pltpu
from jax.sharding import PartitionSpec as P

DK = 256
DV = 512
CH = 256
BLK = 128
NEG_FILL = -1e30
TAIL = 8
ROWS = DK + TAIL
CHUNKS = ((0, 0, DV // 2), (0, DV // 2, DV // 2), (1, 0, DV), (2, 0, DV), (3, 0, DV))
ORDER = (
    (0, 0), (0, 1), (0, 2), (1, 0), (1, 1), (0, 3), (1, 2), (2, 1), (0, 4), (1, 3), (2, 0), (3, 0), (3, 1), (2, 2),
    (4, 0), (1, 4), (3, 2), (4, 1), (5, 0), (2, 3), (3, 3), (5, 1), (4, 2), (2, 4), (3, 4), (4, 3), (6, 0), (6, 1),
    (4, 4), (5, 3), (6, 2), (5, 2), (6, 3),
)

F32 = jnp.float32
BF16 = jnp.bfloat16


def sizes(mesh):
    ctx, head = mesh.shape["ctx"], mesh.shape["head"]
    head_bits, ctx_bits = head.bit_length() - 1, ctx.bit_length() - 1
    assert head == 1 << head_bits and ctx == 1 << ctx_bits and head_bits >= 1
    return head_bits, ctx_bits


def flip(x, bit, head_bits, ctx_bits, last):
    axis, size, b = (
        ("head", 1 << head_bits, bit) if bit < head_bits else ("ctx", 1 << ctx_bits, bit - head_bits)
    )
    pairs = [(i, i ^ (1 << b)) for i in range(size) if not (last and i & (1 << b))]
    return lax.ppermute(x, axis, pairs)


def table_rows(blocks):
    at = {"scale": 0, "row": 3 * blocks, DK: 6 * blocks, DV: 7 * blocks, "factor": 8 * blocks, "peak": 9 * blocks}
    return at, 9 * blocks + 2


def gate_kernel(i_ref, f_ref, scales, tensors, offsets, fbits, run_ref, weight_ref, shift_ref, table_ref):
    gate, x = i_ref[...], f_ref[...].astype(F32)
    log_forget = jnp.minimum(x, 0.0) - jnp.log1p(jnp.exp(-jnp.abs(x)))
    size = x.shape[1]
    row = lax.broadcasted_iota(jnp.int32, (size, size), 0)
    col = lax.broadcasted_iota(jnp.int32, (size, size), 1)
    before = jnp.where(row >= col, 1.0, 0.0).astype(F32)
    same = jnp.where(row == col, 1.0, 0.0).astype(BF16)
    exact = dict(precision=lax.Precision.HIGHEST, preferred_element_type=F32)
    across = (((1,), (1,)), ((), ()))
    running_row = lax.dot_general(log_forget, before, across, **exact)
    running = lax.dot_general(before, log_forget, across, **exact)
    gate_col = lax.dot_general(same, gate, across, preferred_element_type=F32)
    total = running[size - 1 : size, :]
    exponent = total - running + gate_col
    peak = jnp.max(exponent, axis=0, keepdims=True)
    run_ref[...] = running
    weight_ref[...] = jnp.exp(exponent - peak)
    shift_ref[...] = gate.astype(F32) - running_row
    blocks = tensors.shape[0]
    at, _ = table_rows(blocks)
    offset = offsets[...]
    for e in range(3):
        table_ref[at["scale"] + e * blocks : at["scale"] + (e + 1) * blocks, :] = scales[e]
        struck = jnp.where(tensors[...] == e, lax.shift_right_logical(offset, DV.bit_length() - 1), -1)
        table_ref[at["row"] + e * blocks : at["row"] + (e + 1) * blocks, :] = struck.astype(F32)
    for width in (DK, DV):
        table_ref[at[width] : at[width] + blocks, :] = (offset & (width - 1)).astype(F32)
    table_ref[at["factor"] : at["factor"] + blocks, :] = -(lax.shift_left(jnp.ones_like(offset), fbits[...]).astype(F32))
    table_ref[at["peak"] :, :] = jnp.concatenate([peak, total], axis=0)


def gates(input_gate, forget_gate, small):
    heads, size = input_gate.shape
    col = jax.ShapeDtypeStruct((size, heads), F32)
    row = jax.ShapeDtypeStruct((heads, size), F32)
    return pl.pallas_call(
        gate_kernel,
        out_shape=(col, col, row, jax.ShapeDtypeStruct((table_rows(small[1].shape[0])[1], heads), F32)),
        compiler_params=pltpu.CompilerParams(vmem_limit_bytes=4 << 20),
        cost_estimate=pl.CostEstimate(flops=1 << 20, bytes_accessed=1 << 20, transcendentals=0),
        name="gates",
    )(input_gate, forget_gate, *small)


def pick(ref, h):
    x = ref[...]
    lane = lax.broadcasted_iota(jnp.int32, x.shape, 1)
    return jnp.sum(jnp.where(lane == h, x, 0.0), axis=1, keepdims=True)


def dequant(ref, at, lo, width, full, tensor_id, h, table):
    blocks = ref.shape[0] // BLK
    rows, _ = table_rows(blocks)
    row = lax.broadcasted_iota(jnp.int32, (BLK, 1), 0).astype(F32)
    col = (lax.broadcasted_iota(jnp.int32, (1, width), 1) + lo).astype(F32)
    out = []
    for b in range(blocks):
        x = ref[b * BLK : (b + 1) * BLK, pl.ds(pl.multiple_of(at + lo, 128), width)].astype(F32)
        scale = table[rows["scale"] + tensor_id * blocks + b, h]
        hit = (row == table[rows["row"] + tensor_id * blocks + b, h]) & (col == table[rows[full] + b, h])
        out.append((x * jnp.where(hit, table[rows["factor"] + b, h] * scale, scale)).astype(BF16))
    return jnp.concatenate(out, axis=0)


def split(x):
    high = x.astype(BF16).astype(F32)
    middle = (x - high).astype(BF16).astype(F32)
    return high, middle, x - high - middle


def pack_tail(normer, peak, total):
    width = peak.shape[1]
    blank = jnp.zeros((1, width - DK), F32)
    rows = [jnp.concatenate([x, blank], axis=1) if width > DK else x for x in split(normer)[:2]]
    rows += [*split(peak), *split(total)]
    at = lax.broadcasted_iota(jnp.int32, (TAIL, width), 0)
    out = jnp.zeros((TAIL, width), F32)
    for r, value in enumerate(rows):
        out = jnp.where(at == r, value, out)
    return out.astype(BF16)


class State:
    def __init__(self, ref):
        self.ref = ref
        t = ref[DK:ROWS, :].astype(F32)
        self.normer = t[0:1, :DK] + t[1:2, :DK]
        self.peak = t[2:3] + t[3:4] + t[4:5]
        self.total = t[5:6] + t[6:7] + t[7:8]

    def matrix(self):
        return self.ref[:DK, :]


def joined(early, late):
    peak = jnp.maximum(early[0] + late[1], late[0])
    return peak, early[1] + late[1], jnp.exp(early[0] + late[1] - peak), jnp.exp(late[0] - peak)


def group_weights(bit, own, got):
    peak, total, weights = own.peak, own.total, [jnp.ones_like(own.peak)]
    for b, peer in enumerate(got):
        low = joined((peak, total), (peer.peak, peer.total))
        high = joined((peer.peak, peer.total), (peak, total))
        peak, total = jnp.where(bit[b], high[0], low[0]), low[1]
        here, there = jnp.where(bit[b], high[3], low[2]), jnp.where(bit[b], high[2], low[3])
        weights = [w * here for w in weights] + [there]
    return weights, peak, total


def start_weights(bit, include, own, got):
    peak, total, weights = None, None, []
    one = jnp.ones_like(got[-1].peak)
    peak, total = one * NEG_FILL, one * 0.0
    if own is not None:
        peak, total = jnp.where(include, own.peak, peak), jnp.where(include, own.total, total)
        weights = [jnp.where(include, one, 0.0)]
    for b, peer in zip(range(len(bit) - len(got), len(bit)), got):
        new = joined((peer.peak, peer.total), (peak, total))
        weights = [w * jnp.where(bit[b], new[3], 1.0) for w in weights] + [jnp.where(bit[b], new[2], 0.0)]
        peak, total = jnp.where(bit[b], new[0], peak), jnp.where(bit[b], new[1], total)
    return weights, peak, total


def weighted_sum(weights, states):
    matrix, normer = None, None
    for w, state in zip(weights, states):
        term, tail = state.matrix().astype(F32) * w, state.normer * w[:, :DK]
        matrix = term if matrix is None else matrix + term
        normer = tail if normer is None else normer + tail
    return matrix, normer


def device_bits(head_bits, bits):
    me = lax.axis_index("ctx") * (1 << head_bits) + lax.axis_index("head")
    return [((me >> b) & 1) == 1 for b in range(bits)]


def ordered(kernel, operands, after):
    if after is None:
        return kernel, [], []
    at = operands

    def run(*refs):
        kernel(*refs[:at], *refs[at + 1 :])

    return run, [after], [pl.BlockSpec(memory_space=pl.ANY)]


def in_hbm(x):
    return pltpu.with_memory_space_constraint(x, pltpu.HBM)


SMEM = pl.BlockSpec(memory_space=pltpu.SMEM)
VMEM = pl.BlockSpec(memory_space=pltpu.VMEM)


def state_kernel(pair, lo, at, table, weight_ref, k_ref, v_ref, keep_ref, send_ref):
    own = lax.axis_index("head") & 1
    width = keep_ref.shape[1]
    peak_row = table_rows(k_ref.shape[0] // BLK)[0]["peak"]
    for out_ref, side in ((send_ref, 1 - own), (keep_ref, own)):
        h = 2 * pair + side
        k = dequant(k_ref, pl.multiple_of((at + side) * DK, DK), 0, DK, DK, 1, h, table)
        v = dequant(v_ref, pl.multiple_of((at + side) * DV, DV), lo, width, DV, 2, h, table)
        weighted = (k.astype(F32) * pick(weight_ref, h)).astype(BF16)
        matrix = lax.dot_general(weighted, v, (((0,), (0,)), ((), ())), preferred_element_type=F32)
        out_ref[:DK, :] = matrix.astype(BF16)
        normer = jnp.sum(weighted.astype(F32), axis=0, keepdims=True)
        peak = jnp.full((1, width), table[peak_row, h], F32)
        total = jnp.full((1, width), table[peak_row + 1, h], F32)
        out_ref[DK:ROWS, :] = pack_tail(normer, peak, total)


def span_states(chunk, table, weight, key_codes, value_codes, after):
    pair, lo, width = chunk
    rows = key_codes.shape[0]
    out = jax.ShapeDtypeStruct((ROWS, width), BF16)
    if after is None:
        at = 0
        spec = dict(
            grid=(1,),
            in_specs=[SMEM, VMEM]
            + [pl.BlockSpec((rows, 2 * DK), lambda i: (0, pair)), pl.BlockSpec((rows, 2 * DV), lambda i: (0, pair))],
        )
        key_codes, value_codes = in_hbm(key_codes), in_hbm(value_codes)
    else:
        at = 2 * pair
        spec = dict(in_specs=[SMEM, VMEM, VMEM, VMEM])
    kernel, extra, extra_specs = ordered(functools.partial(state_kernel, pair, lo, at), 4, after)
    spec["in_specs"] += extra_specs
    return pl.pallas_call(
        kernel,
        **spec,
        out_specs=(VMEM,) * 2,
        out_shape=(out, out),
        compiler_params=pltpu.CompilerParams(vmem_limit_bytes=12 << 20),
        cost_estimate=pl.CostEstimate(
            flops=4 * rows * DK * width, bytes_accessed=rows * 2 * (2 * DK + 4 * DV), transcendentals=0
        ),
        name="span_states",
    )(table, weight, key_codes, value_codes, *extra)


def combine_kernel(head_bits, bits, last, *refs):
    parts, out_ref = refs[:-1], refs[-1]
    bit = device_bits(head_bits, bits)
    states = [State(ref) for ref in parts]
    if last:
        weights, peak, total = start_weights(bit, jnp.logical_not(bit[0]), states[0], states[1:])
    else:
        weights, peak, total = group_weights(bit, states[0], states[1:])
    matrix, normer = weighted_sum(weights, states)
    out_ref[:DK, :] = matrix.astype(BF16)
    out_ref[DK:ROWS, :] = pack_tail(normer, peak, total)


def combine(head_bits, bits, last, parts, after):
    size = parts[0].size
    kernel, extra, extra_specs = ordered(functools.partial(combine_kernel, head_bits, bits, last), len(parts), after)
    return pl.pallas_call(
        kernel,
        in_specs=[VMEM] * len(parts) + extra_specs,
        out_specs=VMEM,
        out_shape=jax.ShapeDtypeStruct(parts[0].shape, BF16),
        compiler_params=pltpu.CompilerParams(vmem_limit_bytes=8 << 20),
        cost_estimate=pl.CostEstimate(
            flops=size * 2 * len(parts), bytes_accessed=size * 2 * (len(parts) + 1), transcendentals=0
        ),
        name="combine",
    )(*parts, *extra)


def output_kernel(head_bits, bits, pair, mine, pieces, table, run_ref, shift_ref, q_ref, k_ref, v_ref, *rest):
    count = len(rest[:-4]) // pieces
    groups = [rest[p * count : (p + 1) * count] for p in range(pieces)]
    out_ref, token_ref, result_ref, sem = rest[-4:]
    token_ref[...] = jnp.zeros_like(token_ref)
    bit = device_bits(head_bits, bits)
    own = lax.axis_index("head") & 1
    h = 2 * pair + (own if mine else 1 - own)
    narrow, wide = pl.multiple_of(h * DK, DK), pl.multiple_of(h * DV, DV)
    factor = 1.0 / math.sqrt(DK)
    size = q_ref.shape[0]
    row = lax.broadcasted_iota(jnp.int32, (size, size), 0)
    col = lax.broadcasted_iota(jnp.int32, (size, size), 1)
    starts = []
    for group in groups:
        states = [State(ref) for ref in group]
        if mine:
            weights, peak, _ = start_weights(bit, None, None, states)
            start, normer = weighted_sum(weights, states)
            starts.append(start.astype(BF16))
        else:
            normer, peak = states[0].normer, states[0].peak
            starts.append(states[0].matrix())
    start = jnp.concatenate(starts, axis=1) if pieces > 1 else starts[0]
    q = dequant(q_ref, narrow, 0, DK, DK, 0, h, table)
    k = dequant(k_ref, narrow, 0, DK, DK, 1, h, table)
    v = dequant(v_ref, wide, 0, DV, DV, 2, h, table)
    run = pick(run_ref, h)
    exponent = jnp.where(row >= col, run + shift_ref[pl.ds(h, 1), :], NEG_FILL)
    inter = run + peak[:, :1]
    row_peak = jnp.maximum(jnp.max(exponent, axis=1, keepdims=True), inter)
    decay = jnp.exp(exponent - row_peak)
    scores = lax.dot_general(q, k, (((1,), (1,)), ((), ())), preferred_element_type=F32) * factor
    product = decay * scores
    lifted = (q.astype(F32) * (factor * jnp.exp(inter - row_peak))).astype(BF16)
    numerator = jnp.dot(product.astype(BF16), v, preferred_element_type=F32)
    numerator = numerator + jnp.dot(lifted, start, preferred_element_type=F32)
    denominator = jnp.sum(product, axis=1, keepdims=True) + jnp.sum(lifted.astype(F32) * normer, axis=1, keepdims=True)
    result_ref[...] = (numerator / jnp.maximum(jnp.abs(denominator), 1.0)).astype(BF16)
    write = pltpu.make_async_copy(result_ref, out_ref.at[:, pl.ds(wide, DV)], sem)
    write.start()
    write.wait()


def span_outputs(head_bits, bits, pair, mine, table, run, shift, codes, groups, before, after):
    rows, width = codes[2].shape
    states = [x for group in groups for x in group]
    operands = [table, run, shift, *codes, *states]
    in_specs = [SMEM] + [VMEM] * (len(operands) - 1)
    kernel = functools.partial(output_kernel, head_bits, bits, pair, mine, len(groups))
    kernel, extra, extra_specs = ordered(kernel, len(operands), after)
    operands += extra
    in_specs += extra_specs
    aliases = {}
    if before is not None:
        kernel, extra, extra_specs = ordered(kernel, len(operands), before)
        aliases = {len(operands): 0}
        operands += extra
        in_specs += extra_specs
    return pl.pallas_call(
        kernel,
        in_specs=in_specs,
        out_specs=(pl.BlockSpec(memory_space=pl.ANY), VMEM),
        out_shape=(jax.ShapeDtypeStruct((rows, width), BF16), jax.ShapeDtypeStruct((8, 128), F32)),
        scratch_shapes=[pltpu.VMEM((rows, DV), BF16), pltpu.SemaphoreType.DMA],
        input_output_aliases=aliases,
        compiler_params=pltpu.CompilerParams(vmem_limit_bytes=12 << 20),
        cost_estimate=pl.CostEstimate(
            flops=2 * rows * (rows * DK + rows * DV + DK * DV),
            bytes_accessed=rows * 2 * (2 * DK + 2 * DV) + sum(x.size for x in states) * 2,
            transcendentals=rows * rows,
        ),
        name="span_outputs",
    )(*operands)


def body(
    head_bits,
    ctx_bits,
    query_codes,
    key_codes,
    value_codes,
    block_scales,
    fault_tensor,
    fault_offset,
    fault_bit,
    input_gate,
    forget_gate,
):
    bits = head_bits + ctx_bits
    assert query_codes.shape[0] == CH
    assert sum(width for _, _, width in CHUNKS) * 2 == value_codes.shape[1]
    small = tuple(in_hbm(x) for x in (block_scales.transpose(1, 0, 2), fault_tensor, fault_offset, fault_bit))
    codes = (query_codes, key_codes, value_codes)
    exchange = functools.partial(flip, head_bits=head_bits, ctx_bits=ctx_bits)
    run, weight, shift, table = gates(in_hbm(input_gate.T), in_hbm(forget_gate.T), small)
    keep, got, back = {}, {}, {}
    out = token = None
    for stage, c in order(bits):
        if stage == 0:
            keep[c], token = span_states(CHUNKS[c], table, weight, key_codes, value_codes, token)
        elif stage < bits:
            token = combine(head_bits, bits, False, [keep[c], *got[c]], token)
        elif stage == bits:
            token = combine(head_bits, bits, True, [keep[c], *got[c][1:]], token)
        else:
            mine = stage == bits + 1
            groups = [got[d] if mine else [back[d]] for d in of_pair(c)]
            out, token = span_outputs(
                head_bits, bits, c, mine, table, run, shift, codes, groups, out, token
            )
        if stage < bits:
            got.setdefault(c, []).append(exchange(token, stage, last=stage == bits - 1))
        elif stage == bits:
            back[c] = exchange(token, 0, last=False)
    return out


def of_pair(pair):
    return [c for c, chunk in enumerate(CHUNKS) if chunk[0] == pair]


def order(bits):
    stages = {0: [0], 1: [1], 2: range(2, bits - 1), 3: [bits - 1], 4: [bits], 5: [bits + 1], 6: [bits + 2]}
    return [(stage, c) for place, c in ORDER for stage in stages[place]]


def solution(mesh):
    rows = P(("grp", "ctx", "head"), None)
    placed = (rows, rows, rows, P(("grp", "ctx", "head"), None, None)) + (rows,) * 5
    return jax.shard_map(
        functools.partial(body, *sizes(mesh)), mesh=mesh, in_specs=placed, out_specs=rows, check_vma=False
    )
```

```python
import functools
import math

import jax
import jax.numpy as jnp
from jax import lax
from jax.experimental import pallas as pl
from jax.experimental.pallas import tpu as pltpu
from jax.sharding import PartitionSpec as P

DK = 256
DV = 512
CH = 256
BLK = 128
NEG_FILL = -1e30
TAIL = 8
ROWS = DK + TAIL
CHUNKS = ((0, 0, DV // 2), (0, DV // 2, DV // 2), (1, 0, DV), (2, 0, DV), (3, 0, DV))
ORDER = (
    (0, 0), (0, 1), (0, 2), (1, 0), (1, 1), (0, 3), (1, 2), (2, 1), (0, 4), (1, 3), (2, 0), (3, 0), (3, 1), (2, 2),
    (4, 0), (1, 4), (3, 2), (4, 1), (5, 0), (2, 3), (3, 3), (5, 1), (4, 2), (2, 4), (3, 4), (4, 3), (6, 0), (6, 1),
    (4, 4), (5, 3), (6, 2), (5, 2), (6, 3),
)

F32 = jnp.float32
BF16 = jnp.bfloat16


def sizes(mesh):
    ctx, head = mesh.shape["ctx"], mesh.shape["head"]
    head_bits, ctx_bits = head.bit_length() - 1, ctx.bit_length() - 1
    assert head == 1 << head_bits and ctx == 1 << ctx_bits and head_bits >= 1
    return head_bits, ctx_bits


def flip(x, bit, head_bits, ctx_bits, last):
    axis, size, b = (
        ("head", 1 << head_bits, bit) if bit < head_bits else ("ctx", 1 << ctx_bits, bit - head_bits)
    )
    pairs = [(i, i ^ (1 << b)) for i in range(size) if not (last and i & (1 << b))]
    return lax.ppermute(x, axis, pairs)


def table_rows(blocks):
    at = {"scale": 0, "row": 3 * blocks, DK: 6 * blocks, DV: 7 * blocks, "factor": 8 * blocks, "peak": 9 * blocks}
    return at, 9 * blocks + 2


def gate_kernel(i_ref, f_ref, scales, tensors, offsets, fbits, run_ref, weight_ref, shift_ref, table_ref, rows_ref):
    gate, x = i_ref[...], f_ref[...].astype(F32)
    log_forget = jnp.minimum(x, 0.0) - jnp.log1p(jnp.exp(-jnp.abs(x)))
    size = x.shape[1]
    row = lax.broadcasted_iota(jnp.int32, (size, size), 0)
    col = lax.broadcasted_iota(jnp.int32, (size, size), 1)
    before = jnp.where(row >= col, 1.0, 0.0).astype(F32)
    same = jnp.where(row == col, 1.0, 0.0).astype(BF16)
    exact = dict(precision=lax.Precision.HIGHEST, preferred_element_type=F32)
    across = (((1,), (1,)), ((), ()))
    running_row = lax.dot_general(log_forget, before, across, **exact)
    running = lax.dot_general(before, log_forget, across, **exact)
    gate_col = lax.dot_general(same, gate, across, preferred_element_type=F32)
    total = running[size - 1 : size, :]
    exponent = total - running + gate_col
    peak = jnp.max(exponent, axis=0, keepdims=True)
    run_ref[...] = running
    weight_ref[...] = jnp.exp(exponent - peak)
    shift_ref[...] = gate.astype(F32) - running_row
    blocks = tensors.shape[0]
    at, _ = table_rows(blocks)
    offset = offsets[...]
    for e in range(3):
        rows_ref[at["scale"] + e * blocks : at["scale"] + (e + 1) * blocks, :] = scales[e]
        struck = jnp.where(tensors[...] == e, lax.shift_right_logical(offset, DV.bit_length() - 1), -1)
        rows_ref[at["row"] + e * blocks : at["row"] + (e + 1) * blocks, :] = struck.astype(F32)
    for width in (DK, DV):
        rows_ref[at[width] : at[width] + blocks, :] = (offset & (width - 1)).astype(F32)
    rows_ref[at["factor"] : at["factor"] + blocks, :] = -(lax.shift_left(jnp.ones_like(offset), fbits[...]).astype(F32))
    rows_ref[at["peak"] :, :] = jnp.concatenate([peak, total], axis=0)
    for h in range(table_ref.shape[0]):
        table_ref[h] = jnp.broadcast_to(rows_ref[:, h : h + 1], table_ref.shape[1:])


def gates(input_gate, forget_gate, small):
    heads, size = input_gate.shape
    col = jax.ShapeDtypeStruct((size, heads), F32)
    row = jax.ShapeDtypeStruct((heads, size), F32)
    rows = table_rows(small[1].shape[0])[1]
    return pl.pallas_call(
        gate_kernel,
        out_shape=(col, col, row, jax.ShapeDtypeStruct((heads, rows, 128), F32)),
        scratch_shapes=[pltpu.VMEM((rows, heads), F32)],
        compiler_params=pltpu.CompilerParams(vmem_limit_bytes=4 << 20),
        cost_estimate=pl.CostEstimate(flops=1 << 20, bytes_accessed=1 << 20, transcendentals=0),
        name="gates",
    )(input_gate, forget_gate, *small)


def pick(ref, h):
    x = ref[...]
    lane = lax.broadcasted_iota(jnp.int32, x.shape, 1)
    return jnp.sum(jnp.where(lane == h, x, 0.0), axis=1, keepdims=True)


def across(x, width):
    return jnp.concatenate([x] * (width // x.shape[1]), axis=1)


def dequant(ref, at, lo, width, full, tensor_id, table):
    blocks = ref.shape[0] // BLK
    rows, _ = table_rows(blocks)
    row = lax.broadcasted_iota(jnp.int32, (BLK, 128), 0).astype(F32)
    col = (lax.broadcasted_iota(jnp.int32, (1, width), 1) + lo).astype(F32)

    def entry(r):
        return table[r : r + 1, :]

    out = []
    for b in range(blocks):
        x = ref[b * BLK : (b + 1) * BLK, pl.ds(pl.multiple_of(at + lo, 128), width)].astype(F32)
        scale = entry(rows["scale"] + tensor_id * blocks + b)
        in_row = jnp.where(row == entry(rows["row"] + tensor_id * blocks + b), 1.0, 0.0)
        in_col = jnp.where(col == across(entry(rows[full] + b), width), 1.0, 0.0)
        struck = across(entry(rows["factor"] + b) * scale, width)
        factor = jnp.where(across(in_row, width) * in_col > 0.5, struck, across(scale, width))
        out.append((x * factor).astype(BF16))
    return jnp.concatenate(out, axis=0)


def split(x):
    high = x.astype(BF16).astype(F32)
    middle = (x - high).astype(BF16).astype(F32)
    return high, middle, x - high - middle


def pack_tail(normer, peak, total):
    width = peak.shape[1]
    blank = jnp.zeros((1, width - DK), F32)
    rows = [jnp.concatenate([x, blank], axis=1) if width > DK else x for x in split(normer)[:2]]
    rows += [*split(peak), *split(total)]
    at = lax.broadcasted_iota(jnp.int32, (TAIL, width), 0)
    out = jnp.zeros((TAIL, width), F32)
    for r, value in enumerate(rows):
        out = jnp.where(at == r, value, out)
    return out.astype(BF16)


class State:
    def __init__(self, ref):
        self.ref = ref
        t = ref[DK:ROWS, :].astype(F32)
        self.normer = t[0:1, :DK] + t[1:2, :DK]
        self.peak = t[2:3] + t[3:4] + t[4:5]
        self.total = t[5:6] + t[6:7] + t[7:8]

    def matrix(self):
        return self.ref[:DK, :]


def joined(early, late):
    peak = jnp.maximum(early[0] + late[1], late[0])
    return peak, early[1] + late[1], jnp.exp(early[0] + late[1] - peak), jnp.exp(late[0] - peak)


def group_weights(bit, own, got):
    peak, total, weights = own.peak, own.total, [jnp.ones_like(own.peak)]
    for b, peer in enumerate(got):
        low = joined((peak, total), (peer.peak, peer.total))
        high = joined((peer.peak, peer.total), (peak, total))
        peak, total = jnp.where(bit[b], high[0], low[0]), low[1]
        here, there = jnp.where(bit[b], high[3], low[2]), jnp.where(bit[b], high[2], low[3])
        weights = [w * here for w in weights] + [there]
    return weights, peak, total


def start_weights(bit, include, own, got):
    peak, total, weights = None, None, []
    one = jnp.ones_like(got[-1].peak)
    peak, total = one * NEG_FILL, one * 0.0
    if own is not None:
        peak, total = jnp.where(include, own.peak, peak), jnp.where(include, own.total, total)
        weights = [jnp.where(include, one, 0.0)]
    for b, peer in zip(range(len(bit) - len(got), len(bit)), got):
        new = joined((peer.peak, peer.total), (peak, total))
        weights = [w * jnp.where(bit[b], new[3], 1.0) for w in weights] + [jnp.where(bit[b], new[2], 0.0)]
        peak, total = jnp.where(bit[b], new[0], peak), jnp.where(bit[b], new[1], total)
    return weights, peak, total


def weighted_sum(weights, states):
    matrix, normer = None, None
    for w, state in zip(weights, states):
        term, tail = state.matrix().astype(F32) * w, state.normer * w[:, :DK]
        matrix = term if matrix is None else matrix + term
        normer = tail if normer is None else normer + tail
    return matrix, normer


def device_bits(head_bits, bits):
    me = lax.axis_index("ctx") * (1 << head_bits) + lax.axis_index("head")
    return [((me >> b) & 1) == 1 for b in range(bits)]


def ordered(kernel, operands, after):
    if after is None:
        return kernel, [], []
    at = operands

    def run(*refs):
        kernel(*refs[:at], *refs[at + 1 :])

    return run, [after], [pl.BlockSpec(memory_space=pl.ANY)]


def in_hbm(x):
    return pltpu.with_memory_space_constraint(x, pltpu.HBM)


SMEM = pl.BlockSpec(memory_space=pltpu.SMEM)
VMEM = pl.BlockSpec(memory_space=pltpu.VMEM)


def state_kernel(pair, lo, at, table_ref, weight_ref, k_ref, v_ref, keep_ref, send_ref):
    own = lax.axis_index("head") & 1
    width = keep_ref.shape[1]
    peak_row = table_rows(k_ref.shape[0] // BLK)[0]["peak"]
    for out_ref, side in ((send_ref, 1 - own), (keep_ref, own)):
        h = 2 * pair + side
        table = table_ref.at[h]
        k = dequant(k_ref, pl.multiple_of((at + side) * DK, DK), 0, DK, DK, 1, table[...])
        v = dequant(v_ref, pl.multiple_of((at + side) * DV, DV), lo, width, DV, 2, table[...])
        weighted = (k.astype(F32) * pick(weight_ref, h)).astype(BF16)
        matrix = lax.dot_general(weighted, v, (((0,), (0,)), ((), ())), preferred_element_type=F32)
        out_ref[:DK, :] = matrix.astype(BF16)
        normer = jnp.sum(weighted.astype(F32), axis=0, keepdims=True)
        peak = across(table[peak_row : peak_row + 1, :], width)
        total = across(table[peak_row + 1 : peak_row + 2, :], width)
        out_ref[DK:ROWS, :] = pack_tail(normer, peak, total)


def span_states(chunk, table, weight, key_codes, value_codes, after):
    pair, lo, width = chunk
    rows = key_codes.shape[0]
    out = jax.ShapeDtypeStruct((ROWS, width), BF16)
    if after is None:
        at = 0
        spec = dict(
            grid=(1,),
            in_specs=[VMEM, VMEM]
            + [pl.BlockSpec((rows, 2 * DK), lambda i: (0, pair)), pl.BlockSpec((rows, 2 * DV), lambda i: (0, pair))],
        )
        key_codes, value_codes = in_hbm(key_codes), in_hbm(value_codes)
    else:
        at = 2 * pair
        spec = dict(in_specs=[VMEM] * 4)
    kernel, extra, extra_specs = ordered(functools.partial(state_kernel, pair, lo, at), 4, after)
    spec["in_specs"] += extra_specs
    return pl.pallas_call(
        kernel,
        **spec,
        out_specs=(VMEM,) * 2,
        out_shape=(out, out),
        compiler_params=pltpu.CompilerParams(vmem_limit_bytes=12 << 20),
        cost_estimate=pl.CostEstimate(
            flops=4 * rows * DK * width, bytes_accessed=rows * 2 * (2 * DK + 4 * DV), transcendentals=0
        ),
        name="span_states",
    )(table, weight, key_codes, value_codes, *extra)


def combine_kernel(head_bits, bits, last, *refs):
    parts, out_ref = refs[:-1], refs[-1]
    bit = device_bits(head_bits, bits)
    states = [State(ref) for ref in parts]
    if last:
        weights, peak, total = start_weights(bit, jnp.logical_not(bit[0]), states[0], states[1:])
    else:
        weights, peak, total = group_weights(bit, states[0], states[1:])
    matrix, normer = weighted_sum(weights, states)
    out_ref[:DK, :] = matrix.astype(BF16)
    out_ref[DK:ROWS, :] = pack_tail(normer, peak, total)


def combine(head_bits, bits, last, parts, after):
    size = parts[0].size
    kernel, extra, extra_specs = ordered(functools.partial(combine_kernel, head_bits, bits, last), len(parts), after)
    return pl.pallas_call(
        kernel,
        in_specs=[VMEM] * len(parts) + extra_specs,
        out_specs=VMEM,
        out_shape=jax.ShapeDtypeStruct(parts[0].shape, BF16),
        compiler_params=pltpu.CompilerParams(vmem_limit_bytes=8 << 20),
        cost_estimate=pl.CostEstimate(
            flops=size * 2 * len(parts), bytes_accessed=size * 2 * (len(parts) + 1), transcendentals=0
        ),
        name="combine",
    )(*parts, *extra)


def output_kernel(head_bits, bits, pair, mine, pieces, done, table_ref, run_ref, shift_ref, q_ref, k_ref, v_ref, *rest):
    if done is None:
        parts, earlier, (result_ref,) = rest[:-1], (), rest[-1:]
    else:
        parts, earlier, (out_ref, result_ref, sems) = rest[: -3 - len(done)], rest[-3 - len(done) : -3], rest[-3:]
    own = lax.axis_index("head") & 1

    def write(ref, pair, mine, n):
        at = pl.multiple_of((2 * pair + (own if mine else 1 - own)) * DV, DV)
        return pltpu.make_async_copy(ref, out_ref.at[:, pl.ds(at, DV)], sems.at[n])

    writes = [write(ref, *which, n) for n, (ref, which) in enumerate(zip(earlier, done or ()))]
    for copy in writes:
        copy.start()
    count = len(parts) // pieces
    groups = [parts[p * count : (p + 1) * count] for p in range(pieces)]
    bit = device_bits(head_bits, bits)
    h = 2 * pair + (own if mine else 1 - own)
    table = table_ref.at[h]
    narrow, wide = pl.multiple_of(h * DK, DK), pl.multiple_of(h * DV, DV)
    factor = 1.0 / math.sqrt(DK)
    size = q_ref.shape[0]
    row = lax.broadcasted_iota(jnp.int32, (size, size), 0)
    col = lax.broadcasted_iota(jnp.int32, (size, size), 1)
    starts = []
    for group in groups:
        states = [State(ref) for ref in group]
        if mine:
            weights, peak, _ = start_weights(bit, None, None, states)
            start, normer = weighted_sum(weights, states)
            starts.append(start.astype(BF16))
        else:
            normer, peak = states[0].normer, states[0].peak
            starts.append(states[0].matrix())
    start = jnp.concatenate(starts, axis=1) if pieces > 1 else starts[0]
    q = dequant(q_ref, narrow, 0, DK, DK, 0, table[...])
    k = dequant(k_ref, narrow, 0, DK, DK, 1, table[...])
    v = dequant(v_ref, wide, 0, DV, DV, 2, table[...])
    run = pick(run_ref, h)
    exponent = jnp.where(row >= col, run + shift_ref[pl.ds(h, 1), :], NEG_FILL)
    inter = run + peak[:, :1]
    row_peak = jnp.maximum(jnp.max(exponent, axis=1, keepdims=True), inter)
    decay = jnp.exp(exponent - row_peak)
    scores = lax.dot_general(q, k, (((1,), (1,)), ((), ())), preferred_element_type=F32) * factor
    product = decay * scores
    lifted = (q.astype(F32) * (factor * jnp.exp(inter - row_peak))).astype(BF16)
    numerator = jnp.dot(product.astype(BF16), v, preferred_element_type=F32)
    numerator = numerator + jnp.dot(lifted, start, preferred_element_type=F32)
    denominator = jnp.sum(product, axis=1, keepdims=True) + jnp.sum(lifted.astype(F32) * normer, axis=1, keepdims=True)
    result_ref[...] = (numerator / jnp.maximum(jnp.abs(denominator), 1.0)).astype(BF16)
    if done is not None:
        writes.append(write(result_ref, pair, mine, len(done)))
        writes[-1].start()
        for copy in writes:
            copy.wait()


def span_outputs(head_bits, bits, pair, mine, table, run, shift, codes, groups, done, earlier, after):
    rows, width = codes[2].shape
    operands = [table, run, shift, *codes, *[x for group in groups for x in group], *earlier]
    in_specs = [VMEM] * len(operands)
    kernel = functools.partial(output_kernel, head_bits, bits, pair, mine, len(groups), done)
    kernel, extra, extra_specs = ordered(kernel, len(operands), after)
    result = jax.ShapeDtypeStruct((rows, DV), BF16)
    if done is None:
        outs = dict(out_specs=VMEM, out_shape=result)
    else:
        outs = dict(
            out_specs=pl.BlockSpec(memory_space=pl.ANY),
            out_shape=jax.ShapeDtypeStruct((rows, width), BF16),
            scratch_shapes=[pltpu.VMEM(result.shape, BF16), pltpu.SemaphoreType.DMA((len(done) + 1,))],
        )
    return pl.pallas_call(
        kernel,
        in_specs=in_specs + extra_specs,
        **outs,
        compiler_params=pltpu.CompilerParams(vmem_limit_bytes=12 << 20),
        cost_estimate=pl.CostEstimate(
            flops=2 * rows * (rows * DK + rows * DV + DK * DV),
            bytes_accessed=rows * 2 * (2 * DK + 2 * DV),
            transcendentals=rows * rows,
        ),
        name="span_outputs",
    )(*operands, *extra)


def body(
    head_bits,
    ctx_bits,
    query_codes,
    key_codes,
    value_codes,
    block_scales,
    fault_tensor,
    fault_offset,
    fault_bit,
    input_gate,
    forget_gate,
):
    bits = head_bits + ctx_bits
    assert query_codes.shape[0] == CH
    assert sum(width for _, _, width in CHUNKS) * 2 == value_codes.shape[1]
    small = tuple(in_hbm(x) for x in (block_scales.transpose(1, 0, 2), fault_tensor, fault_offset, fault_bit))
    codes = (query_codes, key_codes, value_codes)
    exchange = functools.partial(flip, head_bits=head_bits, ctx_bits=ctx_bits)
    run, weight, shift, table = gates(in_hbm(input_gate.T), in_hbm(forget_gate.T), small)
    keep, got, back = {}, {}, {}
    results, token = {}, None
    for stage, c in order(bits):
        if stage == 0:
            keep[c], token = span_states(CHUNKS[c], table, weight, key_codes, value_codes, token)
        elif stage < bits:
            token = combine(head_bits, bits, False, [keep[c], *got[c]], token)
        elif stage == bits:
            token = combine(head_bits, bits, True, [keep[c], *got[c][1:]], token)
        else:
            mine = stage == bits + 1
            groups = [got[d] if mine else [back[d]] for d in of_pair(c)]
            final = len(results) == input_gate.shape[1] - 1
            token = span_outputs(
                head_bits, bits, c, mine, table, run, shift, codes, groups,
                tuple(results) if final else None, results.values() if final else (), token,
            )
            results[c, mine] = token
        if stage < bits:
            got.setdefault(c, []).append(exchange(token, stage, last=stage == bits - 1))
        elif stage == bits:
            back[c] = exchange(token, 0, last=False)
    return token


def of_pair(pair):
    return [c for c, chunk in enumerate(CHUNKS) if chunk[0] == pair]


def order(bits):
    stages = {0: [0], 1: [1], 2: range(2, bits - 1), 3: [bits - 1], 4: [bits], 5: [bits + 1], 6: [bits + 2]}
    return [(stage, c) for place, c in ORDER for stage in stages[place]]


def solution(mesh):
    rows = P(("grp", "ctx", "head"), None)
    placed = (rows, rows, rows, P(("grp", "ctx", "head"), None, None)) + (rows,) * 5
    return jax.shard_map(
        functools.partial(body, *sizes(mesh)), mesh=mesh, in_specs=placed, out_specs=rows, check_vma=False
    )
```

```python
import functools
import math

import jax
import jax.numpy as jnp
from jax import lax
from jax.experimental import pallas as pl
from jax.experimental.pallas import tpu as pltpu
from jax.sharding import PartitionSpec as P

DK = 256
DV = 512
CH = 256
BLK = 128
NEG_FILL = -1e30
TAIL = 8
BLOCK = DK
CHUNKS = ((0, 0, DV // 2), (0, DV // 2, DV // 2), (1, 0, DV), (2, 0, DV), (3, 0, DV))
ORDER = (
    (0, 0), (0, 1), (0, 2), (1, 0), (1, 1), (0, 3), (1, 2), (2, 1), (0, 4), (1, 3), (2, 0), (3, 0), (3, 1), (2, 2),
    (4, 0), (1, 4), (3, 2), (4, 1), (5, 0), (2, 3), (3, 3), (5, 1), (4, 2), (2, 4), (3, 4), (4, 3), (6, 0), (6, 1),
    (4, 4), (5, 3), (6, 2), (5, 2), (6, 3),
)

F32 = jnp.float32
BF16 = jnp.bfloat16


def sizes(mesh):
    ctx, head = mesh.shape["ctx"], mesh.shape["head"]
    head_bits, ctx_bits = head.bit_length() - 1, ctx.bit_length() - 1
    assert head == 1 << head_bits and ctx == 1 << ctx_bits and head_bits >= 1
    return head_bits, ctx_bits


def flip(x, bit, head_bits, ctx_bits, last):
    axis, size, b = (
        ("head", 1 << head_bits, bit) if bit < head_bits else ("ctx", 1 << ctx_bits, bit - head_bits)
    )
    pairs = [(i, i ^ (1 << b)) for i in range(size) if not (last and i & (1 << b))]
    return lax.ppermute(x, axis, pairs)


def table_rows(blocks):
    at = {"scale": 0, "row": 3 * blocks, DK: 6 * blocks, DV: 7 * blocks, "factor": 8 * blocks, "peak": 9 * blocks}
    return at, 9 * blocks + 2


def gate_kernel(
    first, i_ref, f_ref, scales, tensors, offsets, fbits, k_hbm, v_hbm,
    run_ref, weight_ref, shift_ref, table_ref, keep_ref, send_ref, rows_ref, k_ref, v_ref, sems,
):
    pair, lo, _ = first
    reads = [
        pltpu.make_async_copy(k_hbm.at[:, pl.ds(2 * pair * DK, 2 * DK)], k_ref, sems.at[0]),
        pltpu.make_async_copy(v_hbm.at[:, pl.ds(2 * pair * DV, 2 * DV)], v_ref, sems.at[1]),
    ]
    for copy in reads:
        copy.start()
    gate, x = i_ref[...], f_ref[...].astype(F32)
    log_forget = jnp.minimum(x, 0.0) - jnp.log1p(jnp.exp(-jnp.abs(x)))
    size = x.shape[1]
    row = lax.broadcasted_iota(jnp.int32, (size, size), 0)
    col = lax.broadcasted_iota(jnp.int32, (size, size), 1)
    before = jnp.where(row >= col, 1.0, 0.0).astype(F32)
    same = jnp.where(row == col, 1.0, 0.0).astype(BF16)
    exact = dict(precision=lax.Precision.HIGHEST, preferred_element_type=F32)
    across = (((1,), (1,)), ((), ()))
    running_row = lax.dot_general(log_forget, before, across, **exact)
    running = lax.dot_general(before, log_forget, across, **exact)
    gate_col = lax.dot_general(same, gate, across, preferred_element_type=F32)
    total = running[size - 1 : size, :]
    exponent = total - running + gate_col
    peak = jnp.max(exponent, axis=0, keepdims=True)
    run_ref[...] = running
    weight_ref[...] = jnp.exp(exponent - peak)
    shift_ref[...] = gate.astype(F32) - running_row
    blocks = tensors.shape[0]
    at, _ = table_rows(blocks)
    offset = offsets[...]
    for e in range(3):
        rows_ref[at["scale"] + e * blocks : at["scale"] + (e + 1) * blocks, :] = scales[e]
        struck = jnp.where(tensors[...] == e, lax.shift_right_logical(offset, DV.bit_length() - 1), -1)
        rows_ref[at["row"] + e * blocks : at["row"] + (e + 1) * blocks, :] = struck.astype(F32)
    for width in (DK, DV):
        rows_ref[at[width] : at[width] + blocks, :] = (offset & (width - 1)).astype(F32)
    rows_ref[at["factor"] : at["factor"] + blocks, :] = -(lax.shift_left(jnp.ones_like(offset), fbits[...]).astype(F32))
    rows_ref[at["peak"] :, :] = jnp.concatenate([peak, total], axis=0)
    for h in range(table_ref.shape[0]):
        table_ref[h] = jnp.broadcast_to(rows_ref[:, h : h + 1], table_ref.shape[1:])
    for copy in reads:
        copy.wait()
    state_kernel(pair, lo, 2 * pair, table_ref, weight_ref, k_ref, v_ref, keep_ref, send_ref)


def gates(input_gate, forget_gate, small, key_codes, value_codes):
    heads, size = input_gate.shape
    col = jax.ShapeDtypeStruct((size, heads), F32)
    row = jax.ShapeDtypeStruct((heads, size), F32)
    rows = table_rows(small[1].shape[0])[1]
    state = state_shape(CHUNKS[ORDER[0][1]])
    return pl.pallas_call(
        functools.partial(gate_kernel, CHUNKS[ORDER[0][1]]),
        in_specs=[VMEM] * (2 + len(small)) + [pl.BlockSpec(memory_space=pl.ANY)] * 2,
        out_specs=(VMEM,) * 6,
        out_shape=(col, col, row, jax.ShapeDtypeStruct((heads, rows, 128), F32), state, state),
        scratch_shapes=[
            pltpu.VMEM((rows, heads), F32),
            pltpu.VMEM((size, 2 * DK), BF16),
            pltpu.VMEM((size, 2 * DV), BF16),
            pltpu.SemaphoreType.DMA((2,)),
        ],
        compiler_params=pltpu.CompilerParams(vmem_limit_bytes=8 << 20),
        cost_estimate=pl.CostEstimate(flops=1 << 27, bytes_accessed=1 << 20, transcendentals=0),
        name="gates",
    )(in_hbm(input_gate), in_hbm(forget_gate), *small, in_hbm(key_codes), in_hbm(value_codes))


def state_shape(chunk):
    return jax.ShapeDtypeStruct((chunk[2] // BLOCK * DK + TAIL, BLOCK), BF16)


def pick(ref, h):
    x = ref[...]
    lane = lax.broadcasted_iota(jnp.int32, x.shape, 1)
    return jnp.sum(jnp.where(lane == h, x, 0.0), axis=1, keepdims=True)


def across(x, width):
    return jnp.concatenate([x] * (width // x.shape[1]), axis=1)


def dequant(ref, at, lo, width, full, tensor_id, table):
    blocks = ref.shape[0] // BLK
    rows, _ = table_rows(blocks)
    row = lax.broadcasted_iota(jnp.int32, (BLK, 128), 0).astype(F32)
    col = (lax.broadcasted_iota(jnp.int32, (1, width), 1) + lo).astype(F32)

    def entry(r):
        return table[r : r + 1, :]

    out = []
    for b in range(blocks):
        x = ref[b * BLK : (b + 1) * BLK, pl.ds(pl.multiple_of(at + lo, 128), width)].astype(F32)
        scale = entry(rows["scale"] + tensor_id * blocks + b)
        in_row = jnp.where(row == entry(rows["row"] + tensor_id * blocks + b), 1.0, 0.0)
        in_col = jnp.where(col == across(entry(rows[full] + b), width), 1.0, 0.0)
        struck = across(entry(rows["factor"] + b) * scale, width)
        factor = jnp.where(across(in_row, width) * in_col > 0.5, struck, across(scale, width))
        out.append((x * factor).astype(BF16))
    return jnp.concatenate(out, axis=0)


def split(x):
    high = x.astype(BF16).astype(F32)
    middle = (x - high).astype(BF16).astype(F32)
    return high, middle, x - high - middle


def pack_tail(normer, peak, total):
    rows = [*split(normer)[:2], *split(peak), *split(total)]
    at = lax.broadcasted_iota(jnp.int32, (TAIL, BLOCK), 0)
    out = jnp.zeros((TAIL, BLOCK), F32)
    for r, value in enumerate(rows):
        out = jnp.where(at == r, value, out)
    return out.astype(BF16)


class State:
    def __init__(self, ref):
        self.ref = ref
        t = ref[-TAIL:, :].astype(F32)
        self.normer = t[0:1] + t[1:2]
        self.peak = t[2:3] + t[3:4] + t[4:5]
        self.total = t[5:6] + t[6:7] + t[7:8]

    def matrix(self):
        return self.ref[:-TAIL, :]


def joined(early, late):
    peak = jnp.maximum(early[0] + late[1], late[0])
    return peak, early[1] + late[1], jnp.exp(early[0] + late[1] - peak), jnp.exp(late[0] - peak)


def group_weights(bit, own, got):
    peak, total, weights = own.peak, own.total, [jnp.ones_like(own.peak)]
    for b, peer in enumerate(got):
        low = joined((peak, total), (peer.peak, peer.total))
        high = joined((peer.peak, peer.total), (peak, total))
        peak, total = jnp.where(bit[b], high[0], low[0]), low[1]
        here, there = jnp.where(bit[b], high[3], low[2]), jnp.where(bit[b], high[2], low[3])
        weights = [w * here for w in weights] + [there]
    return weights, peak, total


def start_weights(bit, include, own, got):
    peak, total, weights = None, None, []
    one = jnp.ones_like(got[-1].peak)
    peak, total = one * NEG_FILL, one * 0.0
    if own is not None:
        peak, total = jnp.where(include, own.peak, peak), jnp.where(include, own.total, total)
        weights = [jnp.where(include, one, 0.0)]
    for b, peer in zip(range(len(bit) - len(got), len(bit)), got):
        new = joined((peer.peak, peer.total), (peak, total))
        weights = [w * jnp.where(bit[b], new[3], 1.0) for w in weights] + [jnp.where(bit[b], new[2], 0.0)]
        peak, total = jnp.where(bit[b], new[0], peak), jnp.where(bit[b], new[1], total)
    return weights, peak, total


def weighted_sum(weights, states):
    matrix, normer = None, None
    for w, state in zip(weights, states):
        term, tail = state.matrix().astype(F32) * w, state.normer * w
        matrix = term if matrix is None else matrix + term
        normer = tail if normer is None else normer + tail
    return matrix, normer


def device_bits(head_bits, bits):
    me = lax.axis_index("ctx") * (1 << head_bits) + lax.axis_index("head")
    return [((me >> b) & 1) == 1 for b in range(bits)]


def ordered(kernel, operands, after):
    if after is None:
        return kernel, [], []
    at = operands

    def run(*refs):
        kernel(*refs[:at], *refs[at + 1 :])

    return run, [after], [pl.BlockSpec(memory_space=pl.ANY)]


def in_hbm(x):
    return pltpu.with_memory_space_constraint(x, pltpu.HBM)


SMEM = pl.BlockSpec(memory_space=pltpu.SMEM)
VMEM = pl.BlockSpec(memory_space=pltpu.VMEM)


def state_kernel(pair, lo, at, table_ref, weight_ref, k_ref, v_ref, keep_ref, send_ref):
    own = lax.axis_index("head") & 1
    width = (keep_ref.shape[0] - TAIL) // DK * BLOCK
    peak_row = table_rows(k_ref.shape[0] // BLK)[0]["peak"]
    for out_ref, side in ((send_ref, 1 - own), (keep_ref, own)):
        h = 2 * pair + side
        table = table_ref.at[h]
        k = dequant(k_ref, pl.multiple_of((h - at) * DK, DK), 0, DK, DK, 1, table[...])
        v = dequant(v_ref, pl.multiple_of((h - at) * DV, DV), lo, width, DV, 2, table[...])
        weighted = (k.astype(F32) * pick(weight_ref, h)).astype(BF16)
        matrix = lax.dot_general(weighted, v, (((0,), (0,)), ((), ())), preferred_element_type=F32)
        for c in range(width // BLOCK):
            out_ref[c * DK : (c + 1) * DK, :] = matrix[:, c * BLOCK : (c + 1) * BLOCK].astype(BF16)
        normer = jnp.sum(weighted.astype(F32), axis=0, keepdims=True)
        peak = across(table[peak_row : peak_row + 1, :], BLOCK)
        total = across(table[peak_row + 1 : peak_row + 2, :], BLOCK)
        out_ref[-TAIL:, :] = pack_tail(normer, peak, total)


def span_states(chunk, table, weight, key_codes, value_codes, after):
    pair, lo, width = chunk
    rows = key_codes.shape[0]
    out = state_shape(chunk)
    kernel, extra, extra_specs = ordered(functools.partial(state_kernel, pair, lo, 0), 4, after)
    return pl.pallas_call(
        kernel,
        in_specs=[VMEM] * 4 + extra_specs,
        out_specs=(VMEM,) * 2,
        out_shape=(out, out),
        compiler_params=pltpu.CompilerParams(vmem_limit_bytes=12 << 20),
        cost_estimate=pl.CostEstimate(
            flops=4 * rows * DK * width, bytes_accessed=rows * 2 * (2 * DK + 4 * DV), transcendentals=0
        ),
        name="span_states",
    )(table, weight, key_codes, value_codes, *extra)


def combine_kernel(head_bits, bits, last, *refs):
    parts, out_ref = refs[:-1], refs[-1]
    bit = device_bits(head_bits, bits)
    states = [State(ref) for ref in parts]
    if last:
        weights, peak, total = start_weights(bit, jnp.logical_not(bit[0]), states[0], states[1:])
    else:
        weights, peak, total = group_weights(bit, states[0], states[1:])
    matrix, normer = weighted_sum(weights, states)
    out_ref[:-TAIL, :] = matrix.astype(BF16)
    out_ref[-TAIL:, :] = pack_tail(normer, peak, total)


def combine(head_bits, bits, last, parts, after):
    size = parts[0].size
    kernel, extra, extra_specs = ordered(functools.partial(combine_kernel, head_bits, bits, last), len(parts), after)
    return pl.pallas_call(
        kernel,
        in_specs=[VMEM] * len(parts) + extra_specs,
        out_specs=VMEM,
        out_shape=jax.ShapeDtypeStruct(parts[0].shape, BF16),
        compiler_params=pltpu.CompilerParams(vmem_limit_bytes=8 << 20),
        cost_estimate=pl.CostEstimate(
            flops=size * 2 * len(parts), bytes_accessed=size * 2 * (len(parts) + 1), transcendentals=0
        ),
        name="combine",
    )(*parts, *extra)


def output_kernel(head_bits, bits, pair, mine, pieces, done, table_ref, run_ref, shift_ref, q_ref, k_ref, v_ref, *rest):
    if done is None:
        parts, earlier, (result_ref,) = rest[:-1], (), rest[-1:]
    else:
        parts, earlier, (out_ref, result_ref, sems) = rest[: -3 - len(done)], rest[-3 - len(done) : -3], rest[-3:]
    own = lax.axis_index("head") & 1

    def write(ref, pair, mine, n):
        at = pl.multiple_of((2 * pair + (own if mine else 1 - own)) * DV, DV)
        return pltpu.make_async_copy(ref, out_ref.at[:, pl.ds(at, DV)], sems.at[n])

    writes = [write(ref, *which, n) for n, (ref, which) in enumerate(zip(earlier, done or ()))]
    for copy in writes:
        copy.start()
    count = len(parts) // pieces
    groups = [parts[p * count : (p + 1) * count] for p in range(pieces)]
    bit = device_bits(head_bits, bits)
    h = 2 * pair + (own if mine else 1 - own)
    table = table_ref.at[h]
    narrow, wide = pl.multiple_of(h * DK, DK), pl.multiple_of(h * DV, DV)
    factor = 1.0 / math.sqrt(DK)
    size = q_ref.shape[0]
    row = lax.broadcasted_iota(jnp.int32, (size, size), 0)
    col = lax.broadcasted_iota(jnp.int32, (size, size), 1)
    starts = []
    for group in groups:
        states = [State(ref) for ref in group]
        if mine:
            weights, peak, _ = start_weights(bit, None, None, states)
            start, normer = weighted_sum(weights, states)
            start = start.astype(BF16)
        else:
            start, normer, peak = states[0].matrix(), states[0].normer, states[0].peak
        starts += [start[c : c + DK] for c in range(0, start.shape[0], DK)]
    start = jnp.concatenate(starts, axis=1)
    q = dequant(q_ref, narrow, 0, DK, DK, 0, table[...])
    k = dequant(k_ref, narrow, 0, DK, DK, 1, table[...])
    v = dequant(v_ref, wide, 0, DV, DV, 2, table[...])
    run = pick(run_ref, h)
    exponent = jnp.where(row >= col, run + shift_ref[pl.ds(h, 1), :], NEG_FILL)
    inter = run + peak[:, :1]
    row_peak = jnp.maximum(jnp.max(exponent, axis=1, keepdims=True), inter)
    decay = jnp.exp(exponent - row_peak)
    scores = lax.dot_general(q, k, (((1,), (1,)), ((), ())), preferred_element_type=F32) * factor
    product = decay * scores
    lifted = (q.astype(F32) * (factor * jnp.exp(inter - row_peak))).astype(BF16)
    numerator = jnp.dot(product.astype(BF16), v, preferred_element_type=F32)
    numerator = numerator + jnp.dot(lifted, start, preferred_element_type=F32)
    denominator = jnp.sum(product, axis=1, keepdims=True) + jnp.sum(lifted.astype(F32) * normer, axis=1, keepdims=True)
    result_ref[...] = (numerator / jnp.maximum(jnp.abs(denominator), 1.0)).astype(BF16)
    if done is not None:
        writes.append(write(result_ref, pair, mine, len(done)))
        writes[-1].start()
        for copy in writes:
            copy.wait()


def span_outputs(head_bits, bits, pair, mine, table, run, shift, codes, groups, done, earlier, out, after):
    rows, width = codes[2].shape
    operands = [table, run, shift, *codes, *[x for group in groups for x in group], *earlier]
    in_specs = [VMEM] * len(operands)
    kernel = functools.partial(output_kernel, head_bits, bits, pair, mine, len(groups), done)
    for x in (after, out):
        kernel, extra, extra_specs = ordered(kernel, len(operands), x)
        operands += extra
        in_specs += extra_specs
    result = jax.ShapeDtypeStruct((rows, DV), BF16)
    if done is None:
        outs = dict(out_specs=VMEM, out_shape=result)
    else:
        outs = dict(
            out_specs=pl.BlockSpec(memory_space=pl.ANY),
            out_shape=jax.ShapeDtypeStruct((rows, width), BF16),
            scratch_shapes=[pltpu.VMEM(result.shape, BF16), pltpu.SemaphoreType.DMA((len(done) + 1,))],
            input_output_aliases={} if out is None else {len(operands) - 1: 0},
        )
    return pl.pallas_call(
        kernel,
        in_specs=in_specs,
        **outs,
        compiler_params=pltpu.CompilerParams(vmem_limit_bytes=12 << 20),
        cost_estimate=pl.CostEstimate(
            flops=2 * rows * (rows * DK + rows * DV + DK * DV),
            bytes_accessed=rows * 2 * (2 * DK + 2 * DV),
            transcendentals=rows * rows,
        ),
        name="span_outputs",
    )(*operands)


def body(
    head_bits,
    ctx_bits,
    query_codes,
    key_codes,
    value_codes,
    block_scales,
    fault_tensor,
    fault_offset,
    fault_bit,
    input_gate,
    forget_gate,
):
    bits = head_bits + ctx_bits
    assert query_codes.shape[0] == CH
    assert sum(width for _, _, width in CHUNKS) * 2 == value_codes.shape[1]
    small = tuple(in_hbm(x) for x in (block_scales.transpose(1, 0, 2), fault_tensor, fault_offset, fault_bit))
    codes = (query_codes, key_codes, value_codes)
    exchange = functools.partial(flip, head_bits=head_bits, ctx_bits=ctx_bits)
    keep, got, back = {}, {}, {}
    results, out, token = {}, None, None
    for stage, c in order(bits):
        if not keep:
            run, weight, shift, table, keep[c], token = gates(
                input_gate.T, forget_gate.T, small, key_codes, value_codes
            )
        elif stage == 0:
            keep[c], token = span_states(CHUNKS[c], table, weight, key_codes, value_codes, token)
        elif stage < bits:
            token = combine(head_bits, bits, False, [keep[c], *got[c]], token)
        elif stage == bits:
            token = combine(head_bits, bits, True, [keep[c], *got[c][1:]], token)
        else:
            mine = stage == bits + 1
            groups = [got[d] if mine else [back[d]] for d in of_pair(c)]
            left = input_gate.shape[1] - len(results)
            done = tuple(results) if left == 2 else () if left == 1 else None
            earlier = results.values() if left == 2 else ()
            token = span_outputs(head_bits, bits, c, mine, table, run, shift, codes, groups, done, earlier, out, token)
            results[c, mine] = token
            out, token = (token, None) if done is not None else (None, token)
        if stage < bits:
            got.setdefault(c, []).append(exchange(token, stage, last=stage == bits - 1))
        elif stage == bits:
            back[c] = exchange(token, 0, last=False)
    return out


def of_pair(pair):
    return [c for c, chunk in enumerate(CHUNKS) if chunk[0] == pair]


def order(bits):
    stages = {0: [0], 1: [1], 2: range(2, bits - 1), 3: [bits - 1], 4: [bits], 5: [bits + 1], 6: [bits + 2]}
    return [(stage, c) for place, c in ORDER for stage in stages[place]]


def solution(mesh):
    rows = P(("grp", "ctx", "head"), None)
    placed = (rows, rows, rows, P(("grp", "ctx", "head"), None, None)) + (rows,) * 5
    return jax.shard_map(
        functools.partial(body, *sizes(mesh)), mesh=mesh, in_specs=placed, out_specs=rows, check_vma=False
    )
```

```python
import functools
import math

import jax
import jax.numpy as jnp
from jax import lax
from jax.experimental import pallas as pl
from jax.experimental.pallas import tpu as pltpu
from jax.sharding import PartitionSpec as P

DK = 256
DV = 512
CH = 256
BLK = 128
NEG_FILL = -1e30
TAIL = 8
BLOCK = DK
CHUNKS = ((0, 0, DV // 2), (0, DV // 2, DV // 2), (1, 0, DV), (2, 0, DV), (3, 0, DV))
ORDER = (
    (0, 0), (0, 1), (0, 2), (1, 0), (1, 1), (0, 3), (1, 2), (2, 1), (0, 4), (1, 3), (2, 0), (3, 0), (3, 1), (2, 2),
    (4, 0), (1, 4), (3, 2), (4, 1), (5, 0), (2, 3), (3, 3), (5, 1), (4, 2), (2, 4), (3, 4), (4, 3), (6, 0), (6, 1),
    (4, 4), (5, 3), (6, 2), (5, 2), (6, 3),
)

F32 = jnp.float32
BF16 = jnp.bfloat16


def sizes(mesh):
    ctx, head = mesh.shape["ctx"], mesh.shape["head"]
    head_bits, ctx_bits = head.bit_length() - 1, ctx.bit_length() - 1
    assert head == 1 << head_bits and ctx == 1 << ctx_bits and head_bits >= 1
    return head_bits, ctx_bits


def flip(x, bit, head_bits, ctx_bits):
    axis, size, b = (
        ("head", 1 << head_bits, bit) if bit < head_bits else ("ctx", 1 << ctx_bits, bit - head_bits)
    )
    return lax.ppermute(x, axis, [(i, i ^ (1 << b)) for i in range(size)])


def table_rows(blocks):
    at = {"scale": 0, "row": 3 * blocks, DK: 6 * blocks, DV: 7 * blocks, "factor": 8 * blocks, "peak": 9 * blocks}
    return at, 9 * blocks + 2


def gate_kernel(
    first, i_ref, f_ref, scales, tensors, offsets, fbits, k_hbm, v_hbm,
    run_ref, weight_ref, shift_ref, table_ref, keep_ref, send_ref, rows_ref, k_ref, v_ref, sems,
):
    pair, lo, _ = first
    reads = [
        pltpu.make_async_copy(k_hbm.at[:, pl.ds(2 * pair * DK, 2 * DK)], k_ref, sems.at[0]),
        pltpu.make_async_copy(v_hbm.at[:, pl.ds(2 * pair * DV, 2 * DV)], v_ref, sems.at[1]),
    ]
    for copy in reads:
        copy.start()
    gate, x = i_ref[...], f_ref[...].astype(F32)
    log_forget = jnp.minimum(x, 0.0) - jnp.log1p(jnp.exp(-jnp.abs(x)))
    size = x.shape[1]
    row = lax.broadcasted_iota(jnp.int32, (size, size), 0)
    col = lax.broadcasted_iota(jnp.int32, (size, size), 1)
    before = jnp.where(row >= col, 1.0, 0.0).astype(F32)
    same = jnp.where(row == col, 1.0, 0.0).astype(BF16)
    exact = dict(precision=lax.Precision.HIGHEST, preferred_element_type=F32)
    across = (((1,), (1,)), ((), ()))
    running_row = lax.dot_general(log_forget, before, across, **exact)
    running = lax.dot_general(before, log_forget, across, **exact)
    gate_col = lax.dot_general(same, gate, across, preferred_element_type=F32)
    total = running[size - 1 : size, :]
    exponent = total - running + gate_col
    peak = jnp.max(exponent, axis=0, keepdims=True)
    run_ref[...] = running
    weight_ref[...] = jnp.exp(exponent - peak)
    shift_ref[...] = gate.astype(F32) - running_row
    blocks = tensors.shape[0]
    at, _ = table_rows(blocks)
    offset = offsets[...]
    for e in range(3):
        rows_ref[at["scale"] + e * blocks : at["scale"] + (e + 1) * blocks, :] = scales[e]
        struck = jnp.where(tensors[...] == e, lax.shift_right_logical(offset, DV.bit_length() - 1), -1)
        rows_ref[at["row"] + e * blocks : at["row"] + (e + 1) * blocks, :] = struck.astype(F32)
    for width in (DK, DV):
        rows_ref[at[width] : at[width] + blocks, :] = (offset & (width - 1)).astype(F32)
    rows_ref[at["factor"] : at["factor"] + blocks, :] = -(lax.shift_left(jnp.ones_like(offset), fbits[...]).astype(F32))
    rows_ref[at["peak"] :, :] = jnp.concatenate([peak, total], axis=0)
    for h in range(table_ref.shape[0]):
        table_ref[h] = jnp.broadcast_to(rows_ref[:, h : h + 1], table_ref.shape[1:])
    for copy in reads:
        copy.wait()
    state_kernel(pair, lo, 2 * pair, table_ref, weight_ref, k_ref, v_ref, keep_ref, send_ref)


def gates(input_gate, forget_gate, small, key_codes, value_codes):
    heads, size = input_gate.shape
    col = jax.ShapeDtypeStruct((size, heads), F32)
    row = jax.ShapeDtypeStruct((heads, size), F32)
    rows = table_rows(small[1].shape[0])[1]
    state = state_shape(CHUNKS[ORDER[0][1]])
    return pl.pallas_call(
        functools.partial(gate_kernel, CHUNKS[ORDER[0][1]]),
        in_specs=[VMEM] * (2 + len(small)) + [pl.BlockSpec(memory_space=pl.ANY)] * 2,
        out_specs=(VMEM,) * 6,
        out_shape=(col, col, row, jax.ShapeDtypeStruct((heads, rows, 128), F32), state, state),
        scratch_shapes=[
            pltpu.VMEM((rows, heads), F32),
            pltpu.VMEM((size, 2 * DK), BF16),
            pltpu.VMEM((size, 2 * DV), BF16),
            pltpu.SemaphoreType.DMA((2,)),
        ],
        compiler_params=pltpu.CompilerParams(vmem_limit_bytes=8 << 20),
        cost_estimate=pl.CostEstimate(flops=1 << 27, bytes_accessed=1 << 20, transcendentals=0),
        name="gates",
    )(in_hbm(input_gate), in_hbm(forget_gate), *small, in_hbm(key_codes), in_hbm(value_codes))


def state_shape(chunk):
    return jax.ShapeDtypeStruct((chunk[2] // BLOCK * DK + TAIL, BLOCK), BF16)


def pick(ref, h):
    x = ref[...]
    lane = lax.broadcasted_iota(jnp.int32, x.shape, 1)
    return jnp.sum(jnp.where(lane == h, x, 0.0), axis=1, keepdims=True)


def across(x, width):
    return jnp.concatenate([x] * (width // x.shape[1]), axis=1)


def dequant(ref, at, lo, width, full, tensor_id, table):
    blocks = ref.shape[0] // BLK
    rows, _ = table_rows(blocks)
    row = lax.broadcasted_iota(jnp.int32, (BLK, 128), 0).astype(F32)
    col = (lax.broadcasted_iota(jnp.int32, (1, width), 1) + lo).astype(F32)

    def entry(r):
        return table[r : r + 1, :]

    out = []
    for b in range(blocks):
        x = ref[b * BLK : (b + 1) * BLK, pl.ds(pl.multiple_of(at + lo, 128), width)].astype(F32)
        scale = entry(rows["scale"] + tensor_id * blocks + b)
        in_row = jnp.where(row == entry(rows["row"] + tensor_id * blocks + b), 1.0, 0.0)
        in_col = jnp.where(col == across(entry(rows[full] + b), width), 1.0, 0.0)
        struck = across(entry(rows["factor"] + b) * scale, width)
        factor = jnp.where(across(in_row, width) * in_col > 0.5, struck, across(scale, width))
        out.append((x * factor).astype(BF16))
    return jnp.concatenate(out, axis=0)


def split(x):
    high = x.astype(BF16).astype(F32)
    middle = (x - high).astype(BF16).astype(F32)
    return high, middle, x - high - middle


def pack_tail(normer, peak, total):
    rows = [*split(normer)[:2], *split(peak), *split(total)]
    at = lax.broadcasted_iota(jnp.int32, (TAIL, BLOCK), 0)
    out = jnp.zeros((TAIL, BLOCK), F32)
    for r, value in enumerate(rows):
        out = jnp.where(at == r, value, out)
    return out.astype(BF16)


class State:
    def __init__(self, ref):
        self.ref = ref
        t = ref[-TAIL:, :].astype(F32)
        self.normer = t[0:1] + t[1:2]
        self.peak = t[2:3] + t[3:4] + t[4:5]
        self.total = t[5:6] + t[6:7] + t[7:8]

    def matrix(self):
        return self.ref[:-TAIL, :]


def joined(early, late):
    peak = jnp.maximum(early[0] + late[1], late[0])
    return peak, early[1] + late[1], jnp.exp(early[0] + late[1] - peak), jnp.exp(late[0] - peak)


def group_weights(bit, own, got):
    peak, total, weights = own.peak, own.total, [jnp.ones_like(own.peak)]
    for b, peer in enumerate(got):
        low = joined((peak, total), (peer.peak, peer.total))
        high = joined((peer.peak, peer.total), (peak, total))
        peak, total = jnp.where(bit[b], high[0], low[0]), low[1]
        here, there = jnp.where(bit[b], high[3], low[2]), jnp.where(bit[b], high[2], low[3])
        weights = [w * here for w in weights] + [there]
    return weights, peak, total


def start_weights(bit, include, own, got):
    peak, total, weights = None, None, []
    one = jnp.ones_like(got[-1].peak)
    peak, total = one * NEG_FILL, one * 0.0
    if own is not None:
        peak, total = jnp.where(include, own.peak, peak), jnp.where(include, own.total, total)
        weights = [jnp.where(include, one, 0.0)]
    for b, peer in zip(range(len(bit) - len(got), len(bit)), got):
        new = joined((peer.peak, peer.total), (peak, total))
        weights = [w * jnp.where(bit[b], new[3], 1.0) for w in weights] + [jnp.where(bit[b], new[2], 0.0)]
        peak, total = jnp.where(bit[b], new[0], peak), jnp.where(bit[b], new[1], total)
    return weights, peak, total


def weighted_sum(weights, states):
    matrix, normer = None, None
    for w, state in zip(weights, states):
        term, tail = state.matrix().astype(F32) * w, state.normer * w
        matrix = term if matrix is None else matrix + term
        normer = tail if normer is None else normer + tail
    return matrix, normer


def device_bits(head_bits, bits):
    me = lax.axis_index("ctx") * (1 << head_bits) + lax.axis_index("head")
    return [((me >> b) & 1) == 1 for b in range(bits)]


def ordered(kernel, operands, after):
    if after is None:
        return kernel, [], []
    at = operands

    def run(*refs):
        kernel(*refs[:at], *refs[at + 1 :])

    return run, [after], [pl.BlockSpec(memory_space=pl.ANY)]


def in_hbm(x):
    return pltpu.with_memory_space_constraint(x, pltpu.HBM)


SMEM = pl.BlockSpec(memory_space=pltpu.SMEM)
VMEM = pl.BlockSpec(memory_space=pltpu.VMEM)


def state_kernel(pair, lo, at, table_ref, weight_ref, k_ref, v_ref, keep_ref, send_ref):
    own = lax.axis_index("head") & 1
    width = (keep_ref.shape[0] - TAIL) // DK * BLOCK
    peak_row = table_rows(k_ref.shape[0] // BLK)[0]["peak"]
    for out_ref, side in ((send_ref, 1 - own), (keep_ref, own)):
        h = 2 * pair + side
        table = table_ref.at[h]
        k = dequant(k_ref, pl.multiple_of((h - at) * DK, DK), 0, DK, DK, 1, table[...])
        v = dequant(v_ref, pl.multiple_of((h - at) * DV, DV), lo, width, DV, 2, table[...])
        weighted = (k.astype(F32) * pick(weight_ref, h)).astype(BF16)
        matrix = lax.dot_general(weighted, v, (((0,), (0,)), ((), ())), preferred_element_type=F32)
        for c in range(width // BLOCK):
            out_ref[c * DK : (c + 1) * DK, :] = matrix[:, c * BLOCK : (c + 1) * BLOCK].astype(BF16)
        normer = jnp.sum(weighted.astype(F32), axis=0, keepdims=True)
        peak = across(table[peak_row : peak_row + 1, :], BLOCK)
        total = across(table[peak_row + 1 : peak_row + 2, :], BLOCK)
        out_ref[-TAIL:, :] = pack_tail(normer, peak, total)


def span_states(chunk, table, weight, key_codes, value_codes, after):
    pair, lo, width = chunk
    rows = key_codes.shape[0]
    out = state_shape(chunk)
    kernel, extra, extra_specs = ordered(functools.partial(state_kernel, pair, lo, 0), 4, after)
    return pl.pallas_call(
        kernel,
        in_specs=[VMEM] * 4 + extra_specs,
        out_specs=(VMEM,) * 2,
        out_shape=(out, out),
        compiler_params=pltpu.CompilerParams(vmem_limit_bytes=12 << 20),
        cost_estimate=pl.CostEstimate(
            flops=4 * rows * DK * width, bytes_accessed=rows * 2 * (2 * DK + 4 * DV), transcendentals=0
        ),
        name="span_states",
    )(table, weight, key_codes, value_codes, *extra)


def combine_kernel(head_bits, bits, last, *refs):
    parts, out_ref = refs[:-1], refs[-1]
    bit = device_bits(head_bits, bits)
    states = [State(ref) for ref in parts]
    if last:
        weights, peak, total = start_weights(bit, jnp.logical_not(bit[0]), states[0], states[1:])
    else:
        weights, peak, total = group_weights(bit, states[0], states[1:])
    matrix, normer = weighted_sum(weights, states)
    out_ref[:-TAIL, :] = matrix.astype(BF16)
    out_ref[-TAIL:, :] = pack_tail(normer, peak, total)


def combine(head_bits, bits, last, parts, after):
    size = parts[0].size
    kernel, extra, extra_specs = ordered(functools.partial(combine_kernel, head_bits, bits, last), len(parts), after)
    return pl.pallas_call(
        kernel,
        in_specs=[VMEM] * len(parts) + extra_specs,
        out_specs=VMEM,
        out_shape=jax.ShapeDtypeStruct(parts[0].shape, BF16),
        compiler_params=pltpu.CompilerParams(vmem_limit_bytes=8 << 20),
        cost_estimate=pl.CostEstimate(
            flops=size * 2 * len(parts), bytes_accessed=size * 2 * (len(parts) + 1), transcendentals=0
        ),
        name="combine",
    )(*parts, *extra)


def output_kernel(head_bits, bits, pair, mine, pieces, done, table_ref, run_ref, shift_ref, q_ref, k_ref, v_ref, *rest):
    if done is None:
        parts, earlier, (result_ref,) = rest[:-1], (), rest[-1:]
    else:
        parts, earlier, (out_ref, result_ref, sems) = rest[: -3 - len(done)], rest[-3 - len(done) : -3], rest[-3:]
    own = lax.axis_index("head") & 1

    def write(ref, pair, mine, n):
        at = pl.multiple_of((2 * pair + (own if mine else 1 - own)) * DV, DV)
        return pltpu.make_async_copy(ref, out_ref.at[:, pl.ds(at, DV)], sems.at[n])

    writes = [write(ref, *which, n) for n, (ref, which) in enumerate(zip(earlier, done or ()))]
    for copy in writes:
        copy.start()
    count = len(parts) // pieces
    groups = [parts[p * count : (p + 1) * count] for p in range(pieces)]
    bit = device_bits(head_bits, bits)
    h = 2 * pair + (own if mine else 1 - own)
    table = table_ref.at[h]
    narrow, wide = pl.multiple_of(h * DK, DK), pl.multiple_of(h * DV, DV)
    factor = 1.0 / math.sqrt(DK)
    size = q_ref.shape[0]
    row = lax.broadcasted_iota(jnp.int32, (size, size), 0)
    col = lax.broadcasted_iota(jnp.int32, (size, size), 1)
    starts = []
    for group in groups:
        states = [State(ref) for ref in group]
        if mine:
            weights, peak, _ = start_weights(bit, None, None, states)
            start, normer = weighted_sum(weights, states)
            start = start.astype(BF16)
        else:
            start, normer, peak = states[0].matrix(), states[0].normer, states[0].peak
        starts += [start[c : c + DK] for c in range(0, start.shape[0], DK)]
    start = jnp.concatenate(starts, axis=1)
    q = dequant(q_ref, narrow, 0, DK, DK, 0, table[...])
    k = dequant(k_ref, narrow, 0, DK, DK, 1, table[...])
    v = dequant(v_ref, wide, 0, DV, DV, 2, table[...])
    run = pick(run_ref, h)
    exponent = jnp.where(row >= col, run + shift_ref[pl.ds(h, 1), :], NEG_FILL)
    inter = run + peak[:, :1]
    row_peak = jnp.maximum(jnp.max(exponent, axis=1, keepdims=True), inter)
    decay = jnp.exp(exponent - row_peak)
    scores = lax.dot_general(q, k, (((1,), (1,)), ((), ())), preferred_element_type=F32) * factor
    product = decay * scores
    lifted = (q.astype(F32) * (factor * jnp.exp(inter - row_peak))).astype(BF16)
    numerator = jnp.dot(product.astype(BF16), v, preferred_element_type=F32)
    numerator = numerator + jnp.dot(lifted, start, preferred_element_type=F32)
    denominator = jnp.sum(product, axis=1, keepdims=True) + jnp.sum(lifted.astype(F32) * normer, axis=1, keepdims=True)
    result_ref[...] = (numerator / jnp.maximum(jnp.abs(denominator), 1.0)).astype(BF16)
    if done is not None:
        writes.append(write(result_ref, pair, mine, len(done)))
        writes[-1].start()
        for copy in writes:
            copy.wait()


def span_outputs(head_bits, bits, pair, mine, table, run, shift, codes, groups, done, earlier, out, after):
    rows, width = codes[2].shape
    operands = [table, run, shift, *codes, *[x for group in groups for x in group], *earlier]
    in_specs = [VMEM] * len(operands)
    kernel = functools.partial(output_kernel, head_bits, bits, pair, mine, len(groups), done)
    for x in (after, out):
        kernel, extra, extra_specs = ordered(kernel, len(operands), x)
        operands += extra
        in_specs += extra_specs
    result = jax.ShapeDtypeStruct((rows, DV), BF16)
    if done is None:
        outs = dict(out_specs=VMEM, out_shape=result)
    else:
        outs = dict(
            out_specs=pl.BlockSpec(memory_space=pl.ANY),
            out_shape=jax.ShapeDtypeStruct((rows, width), BF16),
            scratch_shapes=[pltpu.VMEM(result.shape, BF16), pltpu.SemaphoreType.DMA((len(done) + 1,))],
            input_output_aliases={} if out is None else {len(operands) - 1: 0},
        )
    return pl.pallas_call(
        kernel,
        in_specs=in_specs,
        **outs,
        compiler_params=pltpu.CompilerParams(vmem_limit_bytes=12 << 20),
        cost_estimate=pl.CostEstimate(
            flops=2 * rows * (rows * DK + rows * DV + DK * DV),
            bytes_accessed=rows * 2 * (2 * DK + 2 * DV),
            transcendentals=rows * rows,
        ),
        name="span_outputs",
    )(*operands)


def body(
    head_bits,
    ctx_bits,
    query_codes,
    key_codes,
    value_codes,
    block_scales,
    fault_tensor,
    fault_offset,
    fault_bit,
    input_gate,
    forget_gate,
):
    bits = head_bits + ctx_bits
    assert query_codes.shape[0] == CH
    assert sum(width for _, _, width in CHUNKS) * 2 == value_codes.shape[1]
    small = tuple(in_hbm(x) for x in (block_scales.transpose(1, 0, 2), fault_tensor, fault_offset, fault_bit))
    codes = (query_codes, key_codes, value_codes)
    exchange = functools.partial(flip, head_bits=head_bits, ctx_bits=ctx_bits)
    keep, got, back = {}, {}, {}
    results, out, token = {}, None, None
    for stage, c in order(bits):
        if not keep:
            run, weight, shift, table, keep[c], token = gates(
                input_gate.T, forget_gate.T, small, key_codes, value_codes
            )
        elif stage == 0:
            keep[c], token = span_states(CHUNKS[c], table, weight, key_codes, value_codes, token)
        elif stage < bits:
            token = combine(head_bits, bits, False, [keep[c], *got[c]], token)
        elif stage == bits:
            token = combine(head_bits, bits, True, [keep[c], *got[c][1:]], token)
        else:
            mine = stage == bits + 1
            groups = [got[d] if mine else [back[d]] for d in of_pair(c)]
            left = input_gate.shape[1] - len(results)
            done = tuple(results) if left == 2 else () if left == 1 else None
            earlier = results.values() if left == 2 else ()
            token = span_outputs(head_bits, bits, c, mine, table, run, shift, codes, groups, done, earlier, out, token)
            results[c, mine] = token
            out, token = (token, None) if done is not None else (None, token)
        if stage < bits:
            got.setdefault(c, []).append(exchange(token, stage))
        elif stage == bits:
            back[c] = exchange(token, 0)
    return out


def of_pair(pair):
    return [c for c, chunk in enumerate(CHUNKS) if chunk[0] == pair]


def order(bits):
    stages = {0: [0], 1: [1], 2: range(2, bits - 1), 3: [bits - 1], 4: [bits], 5: [bits + 1], 6: [bits + 2]}
    return [(stage, c) for place, c in ORDER for stage in stages[place]]


def solution(mesh):
    rows = P(("grp", "ctx", "head"), None)
    placed = (rows, rows, rows, P(("grp", "ctx", "head"), None, None)) + (rows,) * 5
    return jax.shard_map(
        functools.partial(body, *sizes(mesh)), mesh=mesh, in_specs=placed, out_specs=rows, check_vma=False
    )
```
